256 devices in a mesh: group: 32 (over y, x, core), tensor: 8 (over z).
Axes of the slice: x: 4, y: 4, z: 8, core: 2. Of those that a mesh axis runs over, the one named last changes fastest.
Arguments:
- retrieved: bfloat16 [16384, 2, 2560], P('group', None, 'tensor'), may hold values from -6 to 6
- branch_states: bfloat16 [16384, 2, 2560], P('group', None, 'tensor'), may hold values from -62 to 62
- out_grad: bfloat16 [16384, 2, 2560], P('group', None, 'tensor'), may hold values from -6 to 6
- key_weight: bfloat16 [2, 2560, 2560], P(None, None, 'tensor'), may hold values from -0.125 to 0.125
- value_weight: bfloat16 [2560, 2560], P(None, 'tensor'), may hold values from -0.125 to 0.125
- key_grad_acc: float32 [2, 2560, 2560], P(None, 'group', 'tensor'), may hold values from -6 to 6
- value_grad_acc: float32 [2560, 2560], P('group', 'tensor'), may hold values from -6 to 6
- row_index: int32 [16384, 2], P('group'), may hold values from 0 to 8191, as said below
- row_tier: int32 [8192], P('group'), may hold values 0 or 1
- adam_mean: float32 [8192, 2560], P('group', 'tensor'), may hold values from -3 to 3
- adam_second: float32 [8192, 2560], P('group', 'tensor'), may hold values from 0.01 to 1
Outputs:
- key_grad: float32 [2, 2560, 2560], P(None, 'group', 'tensor')
- value_grad: float32 [2560, 2560], P('group', 'tensor')
- new_mean: float32 [8192, 2560], P('group', 'tensor')
- new_second: float32 [8192, 2560], P('group', 'tensor')
- row_step: float32 [8192, 2560], P('group', 'tensor')
The draws below stay inside these ranges and needn't reach their ends.
Inputs may be any that keep to these rules, and one draw needn't show every extreme that they name: `row_index`: rows o * 256 to (o + 1) * 256 - 1 belong to owner o. Of the 1024 entries of each group's 512 tokens, at most 128 belong to one owner, and one owner receives exactly 128 entries from every group.
All inputs are finite; a program needn't handle non-finite values. No bound on the sum of `row_tier` on one device may be relied on, other than what follows from the above.
Results may differ from the reference program's by a relative error of at most 0.0054.
Values may be sent and summed in bfloat16 or wider, within the bound.
A program may use at most 128 MiB of HBM per device.

```python
import math
import jax
import jax.numpy as jnp
from jax import lax

D = 2560
KEYS = 2
NGRAM = 2
TOK = 512
CAP = 128
ROWS = 8192
TOKENS = 16384


def draw_branch_states(key, part):
    sub_keys = jax.random.split(key, 3)
    row_scale = jnp.exp(jax.random.uniform(sub_keys[1], (TOKENS, KEYS, 1), jnp.float32, -1.15, 1.15))
    col_scale = jnp.exp(jax.random.uniform(sub_keys[2], (1, 1, D), jnp.float32, -1.15, 1.15))
    base_noise = jnp.clip(jax.random.normal(sub_keys[0], (TOKENS, KEYS, D), jnp.float32), -6.0, 6.0)
    return (base_noise * row_scale * col_scale).astype(jnp.bfloat16)


def draw_row_index(key, part):
    groups = TOKENS // TOK
    owned_rows = ROWS // groups
    entry_count = TOK * NGRAM
    hot_owner = jax.random.randint(jax.random.fold_in(key, 7), (), 0, groups).astype(jnp.int32)

    def one_group(group_id):
        group_key = jax.random.fold_in(jax.random.fold_in(key, 11), group_id)
        pool_key, order_key, local_key = jax.random.split(group_key, 3)
        slot_pool = jax.random.permutation(pool_key, (groups - 1) * CAP)[:entry_count - CAP].astype(jnp.int32)
        other_owner = slot_pool // CAP
        other_owner = other_owner + (other_owner >= hot_owner).astype(jnp.int32)
        owners = jnp.concatenate([jnp.full((CAP,), 1, jnp.int32) * hot_owner, other_owner])
        owners = jax.random.permutation(order_key, owners)
        local_row = jax.random.randint(local_key, (entry_count,), 0, owned_rows).astype(jnp.int32)
        return (owners * owned_rows + local_row).reshape(TOK, NGRAM)
    result = jax.vmap(one_group)(jnp.arange(groups, dtype=jnp.int32))
    return result.reshape(TOKENS, NGRAM).astype(jnp.int32)


def plant(values, rng, least, largest):
    dims = values.shape
    spot = [jax.random.randint(jax.random.fold_in(rng, axis), (), 0, dims[axis]) for axis in range(len(dims))]
    values = values.at[tuple(spot)].set(least)
    longest = dims.index(max(dims))
    spot[longest] = (spot[longest] + 1) % dims[longest]
    return values.at[tuple(spot)].set(largest)


def levels(stream_key, dims, cuts, least, top_value):
    def one(position, blocks):
        steps = jax.random.uniform(jax.random.fold_in(jax.random.fold_in(stream_key, 6), position), (blocks,), jnp.float32, least / len(cuts), top_value / len(cuts))
        return jnp.repeat(jnp.exp(steps), dims[position] // blocks).reshape((-1,) + (1,) * (len(dims) - position - 1))

    factor_of = one(*cuts[0])
    for cut in cuts[1:]:
        factor_of = factor_of * one(*cut)
    return factor_of


def gaussian(stream_key, extent, deviation, bound, shards=(), kind=jnp.bfloat16):
    values = jax.random.normal(stream_key, extent, jnp.float32) * deviation
    if len(shards) > 0:
        values = levels(stream_key, extent, shards, -0.22, 0.18) * values
    return jnp.clip(values, min=-bound, max=bound).astype(kind)


def setup_inputs(seed: int = 0) -> dict:
    splits = jax.random.split(jax.random.key(seed), 12)
    return {
        "retrieved": gaussian(splits[0], (TOKENS, NGRAM, D), 1.0, 6.0, ((0, 32), (2, 8))),
        "branch_states": draw_branch_states(jax.random.fold_in(splits[11], 71), 0),
        "out_grad": gaussian(splits[2], (TOKENS, KEYS, D), 1.0, 6.0, ((0, 32), (2, 8))),
        "key_weight": gaussian(splits[3], (KEYS, D, D), D ** -0.5, 0.125, ((2, 8),)),
        "value_weight": gaussian(splits[4], (D, D), D ** -0.5, 0.125, ((1, 8),)),
        "key_grad_acc": gaussian(splits[5], (KEYS, D, D), 1.0, 6.0, ((1, 32), (2, 8)), jnp.float32),
        "value_grad_acc": gaussian(splits[6], (D, D), 1.0, 6.0, ((0, 32), (1, 8)), jnp.float32),
        "row_index": draw_row_index(jax.random.fold_in(splits[11], 71), 0),
        "row_tier": plant((jax.random.randint(splits[8], (ROWS,), 0, 4) < 1).astype(jnp.int32), jax.random.fold_in(splits[8], 1), 0, 1),
        "adam_mean": gaussian(splits[9], (ROWS, D), 0.2, 3.0, ((0, 32), (1, 8)), jnp.float32),
        "adam_second": jnp.clip(jnp.exp(math.log(1.0) - 4.6051702 * jax.random.uniform(splits[10], (ROWS, D), jnp.float32) ** levels(splits[10], (ROWS, D), ((0, 32), (1, 8)), -0.2, 0.2)), 0.01, 1.0),
    }


EPS_NORM = 1e-06
EPS_ADAM = 1e-08
FIRST_BIAS = 1.0 - 0.9 ** 10
SECOND_BIAS = 1.0 - 0.95 ** 10

def reference(retrieved, branch_states, out_grad, key_weight, value_weight, key_grad_acc, value_grad_acc, row_index, row_tier, adam_mean, adam_second):
    memory = lax.optimization_barrier(jnp.sum(retrieved.astype(jnp.float32), axis=1)).astype(jnp.bfloat16)
    memory_wide = memory.astype(jnp.float32)
    key_vals = jnp.einsum('td,jdc->tjc', memory_wide, key_weight.astype(jnp.float32))
    values = jnp.dot(memory, value_weight, preferred_element_type=jnp.float32)
    states = branch_states.astype(jnp.float32)
    grads_out = out_grad.astype(jnp.float32)
    state_sq = lax.optimization_barrier(jnp.mean(states * states, axis=-1))
    key_sq = lax.optimization_barrier(jnp.mean(key_vals * key_vals, axis=-1))
    cross_dot = lax.optimization_barrier(jnp.sum(states * key_vals, axis=-1))
    out_dot = lax.optimization_barrier(jnp.sum(grads_out * values[:, None, :], axis=-1))
    root_width = jnp.sqrt(jnp.float32(D))
    state_rs = lax.rsqrt(state_sq + EPS_NORM)
    key_rs = lax.rsqrt(key_sq + EPS_NORM)
    scores = cross_dot * state_rs * key_rs / root_width
    gate_val = jax.nn.sigmoid(scores)
    dscore = out_dot * gate_val * (1.0 - gate_val)
    key_cot = ((key_rs * dscore / root_width)[..., None] * (states * state_rs[..., None] - key_vals * (key_rs * scores / root_width)[..., None])).astype(jnp.bfloat16)
    value_cot = lax.optimization_barrier(jnp.sum(gate_val[..., None] * grads_out, axis=1)).astype(jnp.bfloat16)
    key_cot_wide = key_cot.astype(jnp.float32)
    value_cot_wide = value_cot.astype(jnp.float32)
    key_grad = key_grad_acc + jnp.einsum('td,tjc->jdc', memory_wide, key_cot_wide)
    value_grad = value_grad_acc + jnp.dot(memory.T, value_cot, preferred_element_type=jnp.float32)
    memory_cot = jnp.einsum('tjc,jdc->td', key_cot_wide, key_weight.astype(jnp.float32))
    memory_cot = memory_cot + jnp.dot(value_cot, value_weight.T, preferred_element_type=jnp.float32)
    entry_grad = jnp.repeat(memory_cot, NGRAM, axis=0)
    row_grad = jax.ops.segment_sum(entry_grad, row_index.reshape(-1).astype(jnp.int32), num_segments=ROWS)
    row_sq = lax.optimization_barrier(jnp.mean(row_grad * row_grad, axis=1))
    is_hot = (row_tier == 1)[:, None]
    mean_hot = 0.9 * adam_mean + 0.1 * row_grad
    second_hot = 0.95 * adam_second + 0.05 * row_grad * row_grad
    step_hot = mean_hot / FIRST_BIAS / (jnp.sqrt(second_hot / SECOND_BIAS) + EPS_ADAM)
    step_cold = row_grad * lax.rsqrt(row_sq + EPS_NORM)[:, None]
    new_mean = jnp.where(is_hot, mean_hot, adam_mean)
    new_second = jnp.where(is_hot, second_hot, adam_second)
    row_step = jnp.where(is_hot, step_hot, step_cold)
    return (key_grad, value_grad, new_mean, new_second, row_step)
```

```python
import functools

import jax
import jax.numpy as jnp
from jax import lax
from jax.experimental import pallas as pl
from jax.experimental.pallas import tpu as pltpu
from jax.sharding import PartitionSpec as P

EPS_NORM = 1e-06
EPS_ADAM = 1e-08
FIRST_BIAS = 1.0 - 0.9**10
SECOND_BIAS = 1.0 - 0.95**10

MESH = pl.DeviceIdType.MESH
F32 = jnp.float32
BF16 = jnp.bfloat16
NZ = 8
NX = 4
NY = 4
CHIPS = 16
FEAT = 320
HALF = 160
TOKS = 512
WIDE = 2560
OUTS = 960
GROWS = 80
OROWS = 256

NT = (((1,), (1,)), ((), ()))


class GroupReduce:
    def __init__(self, pos, buf, core_in, ring1_in, ring2_in, sems, rows, split):
        self.y, self.x, self.c, self.z = pos
        self.buf, self.core_in, self.r1, self.r2 = buf, core_in, ring1_in, ring2_in
        (self.cs, self.cr, self.s1, self.q1, self.s2, self.q2) = sems
        self.halves = ((0, split), (split, rows - split))
        c, x, y = self.c, self.x, self.y
        self.pa = x + c * (y - x)
        self.pb = y + c * (x - y)
        self.sent = []

    def chip(self, a, b):
        return lax.rem(a + 4, 4) * (1 + 3 * self.c) + lax.rem(b + 4, 4) * (4 - 3 * self.c)

    def dev(self, along_a, d):
        c = self.c
        dx = (1 - c) if along_a else c
        dy = c if along_a else (1 - c)
        nx = lax.rem(self.x + dx * d + 4, 4)
        ny = lax.rem(self.y + dy * d + 4, 4)
        return ((ny * 4 + nx) * 2 + c, self.z)

    def send(self, src, dst, ssem, rsem, dev):
        cp = pltpu.make_async_remote_copy(
            src_ref=src, dst_ref=dst, send_sem=ssem, recv_sem=rsem, device_id=dev, device_id_type=MESH
        )
        cp.start()
        self.sent.append(cp)
        return cp

    def core_send(self, i):
        partner = ((self.y * 4 + self.x) * 2 + (1 - self.c), self.z)
        self.core_copies = getattr(self, "core_copies", {})
        self.core_copies[i] = self.send(
            self.buf.at[1 - self.c, pl.ds(4 * i, 4)],
            self.core_in.at[pl.ds(4 * i, 4)],
            self.cs.at[i],
            self.cr.at[i],
            partner,
        )

    def core_add(self, i):
        self.core_copies[i].wait_recv()

        def body(k, carry):
            n = 4 * i + k
            self.buf[self.c, n] = (self.buf[self.c, n].astype(F32) + self.core_in[n].astype(F32)).astype(BF16)
            return carry

        lax.fori_loop(0, 4, body, 0)

    def ring1_start(self):
        self.k1 = {}
        for way, d in ((0, 1), (1, -1)):
            dev = self.dev(True, d)
            first = (0, 1) if way == 0 else (2, 3)
            free = (2, 3) if way == 0 else (0, 1)
            for i, b in enumerate(first):
                self.k1[way, 0, i] = self.send(
                    self.buf.at[self.c, self.chip(self.pa + 2, b)],
                    self.r1.at[way, 0, i], self.s1.at[way, 0, i], self.q1.at[way, 0, i], dev,
                )
        for way, d in ((0, 1), (1, -1)):
            dev = self.dev(True, d)
            free = (2, 3) if way == 0 else (0, 1)
            for i, b in enumerate(free):
                self.k1[way, 1, i] = self.send(
                    self.buf.at[self.c, self.chip(self.pa + d, b)],
                    self.r1.at[way, 1, i], self.s1.at[way, 1, i], self.q1.at[way, 1, i], dev,
                )

    def ring1_mid(self):
        for i in range(2):
            for way, d in ((0, 1), (1, -1)):
                dev = self.dev(True, d)
                b = ((0, 1) if way == 0 else (2, 3))[i]
                self.k1[way, 0, i].wait_recv()
                n = self.chip(self.pa + d, b)
                self.buf[self.c, n] = (
                    self.buf[self.c, n].astype(F32) + self.r1[way, 0, i].astype(F32)
                ).astype(BF16)
                self.k1[way, 2, i] = self.send(
                    self.buf.at[self.c, n], self.r1.at[way, 2, i], self.s1.at[way, 2, i], self.q1.at[way, 2, i], dev
                )

    def ring1_end(self):
        for b in range(4):
            i = b % 2
            up = 2 if b < 2 else 1
            down = 1 if b < 2 else 2
            self.k1[0, up, i].wait_recv()
            self.k1[1, down, i].wait_recv()
            n = self.chip(self.pa, b)
            self.buf[self.c, n] = (
                self.buf[self.c, n].astype(F32) + self.r1[0, up, i].astype(F32) + self.r1[1, down, i].astype(F32)
            ).astype(BF16)

    def part(self, ref, half):
        at, size = self.halves[half]
        return ref.at[pl.ds(at, size)]

    def ring2_start(self):
        self.k2 = {}
        for way, d in ((0, 1), (1, -1)):
            dev = self.dev(False, d)
            for step, shift in ((0, 2), (1, d)):
                half = way if step == 0 else 1 - way
                self.k2[way, step] = self.send(
                    self.part(self.buf.at[self.c, self.chip(self.pa, self.pb + shift)], half),
                    self.part(self.r2.at[way, step], half),
                    self.s2.at[way, step], self.q2.at[way, step], dev,
                )

    def ring2_mid(self):
        for way, d in ((0, 1), (1, -1)):
            dev = self.dev(False, d)
            half = way
            at, size = self.halves[half]
            self.k2[way, 0].wait_recv()
            n = self.chip(self.pa, self.pb + d)
            rows = pl.ds(at, size)
            self.buf[self.c, n, rows] = (
                self.buf[self.c, n, rows].astype(F32) + self.r2[way, 0, rows].astype(F32)
            ).astype(BF16)
            self.k2[way, 2] = self.send(
                self.part(self.buf.at[self.c, n], half),
                self.part(self.r2.at[way, 2], half),
                self.s2.at[way, 2], self.q2.at[way, 2], dev,
            )

    def ring2_end(self, half):
        up = 2 if half == 0 else 1
        down = 1 if half == 0 else 2
        self.k2[0, up].wait_recv()
        self.k2[1, down].wait_recv()
        at, size = self.halves[half]
        rows = pl.ds(at, size)
        n = self.chip(self.pa, self.pb)
        return (
            self.buf[self.c, n, rows].astype(F32)
            + self.r2[0, up, rows].astype(F32)
            + self.r2[1, down, rows].astype(F32)
        )

    def drain(self):
        for cp in self.sent:
            cp.wait_send()


def exchange(
    ret_hbm, st_hbm, og_hbm, kw_hbm, vw_hbm, idx_ref,
    wg_out, rg_out, rs_out,
    ret, st, og, kw, vw, wcol, wrow, mem, acc, cot, stat, stat_in, zsend, zrecv, mc, rsum, rsum_in,
    wbuf, wcore, wr1, wr2, dbuf, dcore, dr1, dr2,
    in_sem, ag_s, ag_r, ps_s, ps_r, zs_s, zs_r, rs_s, rs_r,
    wcs, wcr, w1s, w1r, w2s, w2r, dcs, dcr, d1s, d1r, d2s, d2r,
):
    g = lax.axis_index("group")
    z = lax.axis_index("tensor")
    c = lax.rem(g, 2)
    x = lax.rem(lax.div(g, 2), 4)
    y = lax.div(g, 8)
    pos = (y, x, c, z)

    loads = [
        pltpu.make_async_copy(src, dst, in_sem.at[i])
        for i, (src, dst) in enumerate(
            ((ret_hbm, ret), (kw_hbm, kw), (vw_hbm, vw), (st_hbm, st), (og_hbm, og))
        )
    ]
    for cp in loads:
        cp.start()

    wred = GroupReduce(pos, wbuf, wcore, wr1, wr2, (wcs, wcr, w1s, w1r, w2s, w2r), GROWS, 48)
    dred = GroupReduce(pos, dbuf, dcore, dr1, dr2, (dcs, dcr, d1s, d1r, d2s, d2r), FEAT, HALF)

    barrier = pltpu.get_barrier_semaphore()
    peers = [(g, lax.rem(z + o, NZ)) for o in range(1, NZ)]
    peers.append(((y * 4 + x) * 2 + 1 - c, z))
    for along in (True, False):
        for d in (1, -1):
            peers.append(wred.dev(along, d))
    for dev in peers:
        pl.semaphore_signal(barrier, inc=1, device_id=dev, device_id_type=MESH)

    loads[0].wait()

    def block(owner, half=None):
        at = lax.rem(owner + 2 * NZ, NZ) * FEAT
        if half is None:
            return pl.ds(pl.multiple_of(at, 32), FEAT)
        return pl.ds(pl.multiple_of(at + half * HALF, 32), HALF)

    mem[block(z)] = (ret[0].astype(F32) + ret[1].astype(F32)).astype(BF16)
    pl.semaphore_wait(barrier, len(peers))

    sent = []

    def send(src, dst, ssem, rsem, dev):
        cp = pltpu.make_async_remote_copy(
            src_ref=src, dst_ref=dst, send_sem=ssem, recv_sem=rsem, device_id=dev, device_id_type=MESH
        )
        cp.start()
        sent.append(cp)
        return cp

    ways = ((0, 1), (1, -1))
    ag = {}

    def ag_step(s):
        for i in range(2):
            for way, d in ways:
                h = i if way == 0 else 1 - i
                if s == 4 and i == 1:
                    continue
                if s > 1:
                    ag[way, s - 1, h].wait_recv()
                at = mem.at[block(z - d * (s - 1), h)]
                ag[way, s, h] = send(
                    at, at, ag_s.at[way, s - 1, h], ag_r.at[way, s - 1, h], (g, lax.rem(z + d + NZ, NZ))
                )

    def split_weights():
        for k in range(NZ):
            cols = slice(k * FEAT, (k + 1) * FEAT)
            wcol[k, 0:FEAT] = kw[0, :, cols]
            wcol[k, FEAT : 2 * FEAT] = kw[1, :, cols]
            wcol[k, 2 * FEAT :] = vw[:, cols]

    def turn_weights(lo, hi):
        def body(k, carry):
            wrow[k] = jnp.transpose(wcol[k])
            return carry

        lax.fori_loop(lo, hi, body, 0)

    def forward(owner, first=False):
        k = lax.rem(owner + 2 * NZ, NZ)
        rhs = mem[block(owner)]

        def body(j, carry):
            rows = pl.ds(pl.multiple_of(j * FEAT, 32), FEAT)
            val = jnp.dot(wcol[k, rows], rhs, preferred_element_type=F32)
            if first:
                acc[rows] = val
            else:
                acc[rows] += val
            return carry

        lax.fori_loop(0, 3, body, 0)

    ag_step(1)
    loads[1].wait()
    loads[2].wait()
    split_weights()
    ag_step(2)
    forward(z, True)
    forward(z - 1)
    forward(z + 1)
    loads[3].wait()
    loads[4].wait()
    for j in range(2):
        s = st[j].astype(F32)
        stat[j : j + 1] = jnp.sum(s * s, axis=0, keepdims=True)
    turn_weights(0, 2)
    ag_step(3)
    forward(z - 2)
    forward(z + 2)
    turn_weights(2, 5)
    ag_step(4)
    ag[0, 3, 1].wait_recv()
    ag[1, 3, 0].wait_recv()
    forward(z - 3)
    forward(z + 3)
    turn_weights(5, 8)
    ag[0, 4, 0].wait_recv()
    ag[1, 4, 1].wait_recv()
    forward(z + 4)

    for j in range(2):
        s = st[j].astype(F32)
        kv = acc[j * FEAT : (j + 1) * FEAT]
        stat[2 + j : 3 + j] = jnp.sum(kv * kv, axis=0, keepdims=True)
        stat[4 + j : 5 + j] = jnp.sum(s * kv, axis=0, keepdims=True)
        stat[6 + j : 7 + j] = jnp.sum(og[j].astype(F32) * acc[2 * FEAT :], axis=0, keepdims=True)

    ps = [
        send(stat, stat_in.at[o - 1], ps_s.at[o - 1], ps_r.at[o - 1], (g, lax.rem(z + o, NZ)))
        for o in range(1, NZ)
    ]
    total = stat[...]
    for o in range(1, NZ):
        ps[o - 1].wait_recv()
        total = total + stat_in[o - 1]

    root = jnp.sqrt(F32(WIDE))
    value_cot = None
    for j in range(2):
        state_rs = lax.rsqrt(total[j : j + 1] / WIDE + EPS_NORM)
        key_rs = lax.rsqrt(total[2 + j : 3 + j] / WIDE + EPS_NORM)
        scores = total[4 + j : 5 + j] * state_rs * key_rs / root
        gate = jax.nn.sigmoid(scores)
        dscore = total[6 + j : 7 + j] * gate * (1.0 - gate)
        lead = key_rs * dscore / root
        back = key_rs * scores / root
        kv = acc[j * FEAT : (j + 1) * FEAT]
        cot[j * FEAT : (j + 1) * FEAT] = (lead * (st[j].astype(F32) * state_rs - kv * back)).astype(BF16)
        part = gate * og[j].astype(F32)
        value_cot = part if value_cot is None else value_cot + part
    cot[2 * FEAT :] = value_cot.astype(BF16)

    zr = {}

    def term(dest, h):
        k = lax.rem(dest + 2 * NZ, NZ)
        return jnp.dot(wrow[k, h * HALF : (h + 1) * HALF], cot[...], preferred_element_type=F32)

    def z_send(way, s, h):
        d = 1 if way == 0 else -1
        val = term(z + d * (5 - s), h)
        if (way, s - 1, h) in zr:
            zr[way, s - 1, h].wait_recv()
            val = val + zrecv[way, s - 2, h].astype(F32)
        zsend[way, s - 1, h] = val.astype(BF16)
        zr[way, s, h] = send(
            zsend.at[way, s - 1, h], zrecv.at[way, s - 1, h], zs_s.at[way, s - 1, h], zs_r.at[way, s - 1, h],
            (g, lax.rem(z + d + NZ, NZ)),
        )

    def z_pair(s, early):
        for way in (0, 1):
            h = way if not early else 1 - way
            z_send(way, s, h)

    def weight_rows(i):
        def body(k, carry):
            n = 4 * i + 2 * k
            rows = pl.ds(pl.multiple_of(n * 2 * GROWS, 32), 4 * GROWS)
            val = lax.dot_general(mem[rows], cot[...], NT, preferred_element_type=F32).astype(BF16)
            for a in range(2):
                for core in range(2):
                    at = (2 * a + core) * GROWS
                    wbuf[core, n + a] = val[at : at + GROWS]
            return carry

        lax.fori_loop(0, 2, body, 0)
        wred.core_send(i)

    z_pair(1, False)
    z_pair(2, True)
    for i in range(4):
        weight_rows(i)
    z_pair(2, False)
    for i in range(4):
        wred.core_add(i)
    wred.ring1_start()
    z_pair(3, True)
    z_pair(3, False)
    wred.ring1_mid()
    z_pair(4, True)
    z_pair(4, False)
    wred.ring1_end()
    wred.ring2_start()

    last = [term(z, h) for h in range(2)]
    for h in (0, 1):
        zr[0, 4, h].wait_recv()
        zr[1, 4, h].wait_recv()
        mc[h * HALF : (h + 1) * HALF] = (
            last[h] + zrecv[0, 3, h].astype(F32) + zrecv[1, 3, h].astype(F32)
        ).astype(BF16)

    ids = idx_ref[...]

    def dense_rows(i):
        def body(k, carry):
            n = 4 * i + k
            for core in range(2):
                rows = lax.broadcasted_iota(jnp.int32, (OROWS, TOKS), 0) + (2 * n + core) * OROWS
                hits = (rows == ids[0:1]).astype(F32) + (rows == ids[1:2]).astype(F32)
                dbuf[core, n] = lax.dot_general(
                    mc[...], hits.astype(BF16), NT, preferred_element_type=F32
                ).astype(BF16)
            return carry

        lax.fori_loop(0, 4, body, 0)
        dred.core_send(i)

    for i in range(4):
        dense_rows(i)
    wred.ring2_mid()
    for i in range(4):
        dred.core_add(i)
    dred.ring1_start()
    for h in range(2):
        at, size = wred.halves[h]
        wg_out[pl.ds(at, size)] = wred.ring2_end(h)
    dred.ring1_mid()
    dred.ring1_end()
    dred.ring2_start()
    dred.ring2_mid()
    squares = None
    for h in range(2):
        at, size = dred.halves[h]
        val = dred.ring2_end(h)
        rg_out[pl.ds(at, size)] = val
        part = jnp.sum(val * val, axis=0, keepdims=True)
        squares = part if squares is None else squares + part
    rsum[...] = jnp.broadcast_to(squares, rsum.shape)
    rq = [
        send(rsum, rsum_in.at[o - 1], rs_s.at[o - 1], rs_r.at[o - 1], (g, lax.rem(z + o, NZ)))
        for o in range(1, NZ)
    ]
    total = rsum[...]
    for o in range(1, NZ):
        rq[o - 1].wait_recv()
        total = total + rsum_in[o - 1]
    rs_out[...] = total
    for cp in sent:
        cp.wait_send()
    wred.drain()
    dred.drain()


def update(wg, rg, rs, kacc, vacc, tier, mean, second, kgrad, vgrad, mean_out, second_out, step_out):
    for j in range(2):
        kgrad[j] = kacc[j] + wg[:, j * FEAT : (j + 1) * FEAT]
    vgrad[...] = vacc[...] + wg[:, 2 * FEAT :]
    row_grad = rg[...]
    is_hot = jnp.broadcast_to(tier[...] == 1, row_grad.shape)
    old_mean, old_second = mean[...], second[...]
    mean_hot = 0.9 * old_mean + 0.1 * row_grad
    second_hot = 0.95 * old_second + 0.05 * row_grad * row_grad
    step_hot = mean_hot / FIRST_BIAS / (jnp.sqrt(second_hot / SECOND_BIAS) + EPS_ADAM)
    step_cold = row_grad * lax.rsqrt(rs[0:1] / WIDE + EPS_NORM)
    mean_out[...] = jnp.where(is_hot, mean_hot, old_mean)
    second_out[...] = jnp.where(is_hot, second_hot, old_second)
    step_out[...] = jnp.where(is_hot, step_hot, step_cold)


def on_device(
    retrieved, branch_states, out_grad, key_weight, value_weight, key_grad_acc, value_grad_acc,
    row_index, row_tier, adam_mean, adam_second,
):
    by_feature = functools.partial(jnp.transpose, axes=(1, 2, 0))
    any_spec = pl.BlockSpec(memory_space=pl.ANY)
    vmem = pl.BlockSpec(memory_space=pltpu.VMEM)
    dma = pltpu.SemaphoreType.DMA
    wg, rg, rs = pl.pallas_call(
        exchange,
        out_shape=(
            jax.ShapeDtypeStruct((GROWS, OUTS), F32),
            jax.ShapeDtypeStruct((FEAT, OROWS), F32),
            jax.ShapeDtypeStruct((8, OROWS), F32),
        ),
        in_specs=[any_spec] * 5 + [vmem],
        out_specs=[vmem] * 3,
        scratch_shapes=[
            pltpu.VMEM((2, FEAT, TOKS), BF16),
            pltpu.VMEM((2, FEAT, TOKS), BF16),
            pltpu.VMEM((2, FEAT, TOKS), BF16),
            pltpu.VMEM((2, FEAT, WIDE), BF16),
            pltpu.VMEM((FEAT, WIDE), BF16),
            pltpu.VMEM((NZ, OUTS, FEAT), BF16),
            pltpu.VMEM((NZ, FEAT, OUTS), BF16),
            pltpu.VMEM((WIDE, TOKS), BF16),
            pltpu.VMEM((OUTS, TOKS), F32),
            pltpu.VMEM((OUTS, TOKS), BF16),
            pltpu.VMEM((8, TOKS), F32),
            pltpu.VMEM((NZ - 1, 8, TOKS), F32),
            pltpu.VMEM((2, 4, 2, HALF, TOKS), BF16),
            pltpu.VMEM((2, 4, 2, HALF, TOKS), BF16),
            pltpu.VMEM((FEAT, TOKS), BF16),
            pltpu.VMEM((8, OROWS), F32),
            pltpu.VMEM((NZ - 1, 8, OROWS), F32),
            pltpu.VMEM((2, CHIPS, GROWS, OUTS), BF16),
            pltpu.VMEM((CHIPS, GROWS, OUTS), BF16),
            pltpu.VMEM((2, 3, 2, GROWS, OUTS), BF16),
            pltpu.VMEM((2, 3, GROWS, OUTS), BF16),
            pltpu.VMEM((2, CHIPS, FEAT, OROWS), BF16),
            pltpu.VMEM((CHIPS, FEAT, OROWS), BF16),
            pltpu.VMEM((2, 3, 2, FEAT, OROWS), BF16),
            pltpu.VMEM((2, 3, FEAT, OROWS), BF16),
            dma((5,)),
            dma((2, 4, 2)), dma((2, 4, 2)),
            dma((NZ - 1,)), dma((NZ - 1,)),
            dma((2, 4, 2)), dma((2, 4, 2)),
            dma((NZ - 1,)), dma((NZ - 1,)),
            dma((4,)), dma((4,)), dma((2, 3, 2)), dma((2, 3, 2)), dma((2, 3)), dma((2, 3)),
            dma((4,)), dma((4,)), dma((2, 3, 2)), dma((2, 3, 2)), dma((2, 3)), dma((2, 3)),
        ],
        compiler_params=pltpu.CompilerParams(
            collective_id=0, has_side_effects=True, vmem_limit_bytes=66_000_000
        ),
        name="exchange",
    )(
        by_feature(retrieved),
        by_feature(branch_states),
        by_feature(out_grad),
        jnp.transpose(key_weight, (0, 2, 1)),
        value_weight.T,
        row_index.T,
    )
    feat_rows = jax.ShapeDtypeStruct((FEAT, OROWS), F32)
    key_grad, value_grad, new_mean, new_second, row_step = pl.pallas_call(
        update,
        out_shape=(
            jax.ShapeDtypeStruct((2, GROWS, FEAT), F32),
            jax.ShapeDtypeStruct((GROWS, FEAT), F32),
            feat_rows, feat_rows, feat_rows,
        ),
        in_specs=[vmem] * 8,
        out_specs=[vmem] * 5,
        name="update",
    )(
        wg, rg, rs, key_grad_acc, value_grad_acc, row_tier.reshape(1, OROWS), adam_mean.T, adam_second.T
    )
    return key_grad, value_grad, new_mean.T, new_second.T, row_step.T


def solution(mesh):
    return jax.shard_map(
        on_device,
        mesh=mesh,
        in_specs=(
            P("group", None, "tensor"),
            P("group", None, "tensor"),
            P("group", None, "tensor"),
            P(None, None, "tensor"),
            P(None, "tensor"),
            P(None, "group", "tensor"),
            P("group", "tensor"),
            P("group", None),
            P("group"),
            P("group", "tensor"),
            P("group", "tensor"),
        ),
        out_specs=(
            P(None, "group", "tensor"),
            P("group", "tensor"),
            P("group", "tensor"),
            P("group", "tensor"),
            P("group", "tensor"),
        ),
        check_vma=False,
    )
```

```python
import functools

import jax
import jax.numpy as jnp
from jax import lax
from jax.experimental import pallas as pl
from jax.experimental.pallas import tpu as pltpu
from jax.sharding import PartitionSpec as P

EPS_NORM = 1e-06
EPS_ADAM = 1e-08
FIRST_BIAS = 1.0 - 0.9**10
SECOND_BIAS = 1.0 - 0.95**10

MESH = pl.DeviceIdType.MESH
F32 = jnp.float32
BF16 = jnp.bfloat16
NZ = 8
NX = 4
NY = 4
CHIPS = 16
FEAT = 320
HALF = 160
TOKS = 512
WIDE = 2560
OUTS = 960
GROWS = 80
OROWS = 256

NT = (((1,), (1,)), ((), ()))


class GroupReduce:
    def __init__(self, pos, buf, ring1_in, ring2_in, sems):
        self.y, self.x, self.c, self.z = pos
        self.buf, self.r1, self.r2 = buf, ring1_in, ring2_in
        self.s1, self.q1, self.s2, self.q2 = sems
        c, x, y = self.c, self.x, self.y
        self.pa = x + c * (y - x)
        self.pb = y + c * (x - y)
        self.sent = []
        self.k1, self.k2 = {}, {}

    def chip(self, da, i):
        a = lax.rem(self.pa + da + 4, 4)
        b = lax.rem(self.pb + (2, 1, -1, 0)[i] + 4, 4)
        return a * (1 + 3 * self.c) + b * (4 - 3 * self.c)

    def dev(self, along_a, d):
        c = self.c
        dx = (1 - c) if along_a else c
        dy = c if along_a else (1 - c)
        nx = lax.rem(self.x + dx * d + 4, 4)
        ny = lax.rem(self.y + dy * d + 4, 4)
        return ((ny * 4 + nx) * 2 + c, self.z)

    def send(self, src, dst, ssem, rsem, dev):
        cp = pltpu.make_async_remote_copy(
            src_ref=src, dst_ref=dst, send_sem=ssem, recv_sem=rsem, device_id=dev, device_id_type=MESH
        )
        cp.start()
        self.sent.append(cp)
        return cp

    def send1(self, way, step, i):
        d = 1 - 2 * way
        n = self.chip(2 if step == 0 else d, i)
        slot = i % 2
        self.k1[way, step, i] = self.send(
            self.buf.at[n], self.r1.at[way, step, slot], self.s1.at[way, step, slot], self.q1.at[way, step, slot],
            self.dev(True, d),
        )

    def ring1_far(self):
        self.send1(0, 0, 0)
        self.send1(1, 0, 2)
        self.send1(0, 0, 1)
        self.send1(1, 0, 3)

    def ring1_near(self):
        self.send1(0, 1, 2)
        self.send1(1, 1, 0)
        self.send1(1, 1, 1)

    def add(self, n, *terms):
        val = self.buf[n].astype(F32)
        for way, step, slot in terms:
            val = val + self.r1[way, step, slot].astype(F32)
        self.buf[n] = val.astype(BF16)

    def ring1_pass(self):
        for way, i in ((0, 0), (1, 2), (0, 1), (1, 3)):
            self.k1[way, 0, i].wait_recv()
            self.add(self.chip(1 - 2 * way, i), (way, 0, i % 2))
            self.send1(way, 2, i)
        self.send1(0, 1, 3)

    def ring1_end(self, i):
        up, down = (2, 1) if i < 2 else (1, 2)
        self.k1[0, up, i].wait_recv()
        self.k1[1, down, i].wait_recv()
        self.add(self.chip(0, i), (0, up, i % 2), (1, down, i % 2))

    def send2(self, i):
        d = (2, 1, -1)[i]
        self.k2[i] = self.send(
            self.buf.at[self.chip(0, i)], self.r2.at[i], self.s2.at[i], self.q2.at[i], self.dev(False, d)
        )

    def cross(self):
        for i in range(3):
            self.ring1_end(i)
            self.send2(i)

    def ring2_end(self):
        val = self.buf[self.chip(0, 3)].astype(F32)
        for i in range(3):
            self.k2[i].wait_recv()
            val = val + self.r2[i].astype(F32)
        return val

    def drain(self):
        for cp in self.sent:
            cp.wait_send()


def exchange(
    ret_hbm, st_hbm, og_hbm, kw_hbm, vw_hbm, idx_ref,
    wg_out, rg_out, rs_out,
    ret, st, og, kw, vw, wcol, wrow, mem, mem_in, acc, cot, cot_in, stat, stat_in, zsend, zrecv, mc, rsum, rsum_in,
    idx_in, id_cols, hits, wbuf, wr1, wr2, dbuf, dr1, dr2,
    in_sem, ag_s, ag_r, ps_s, ps_r, zs_s, zs_r, rs_s, rs_r, co_s, co_r,
    w1s, w1r, w2s, w2r, d1s, d1r, d2s, d2r,
):
    g = lax.axis_index("group")
    z = lax.axis_index("tensor")
    c = lax.rem(g, 2)
    x = lax.rem(lax.div(g, 2), 4)
    y = lax.div(g, 8)
    pos = (y, x, c, z)

    loads = [
        pltpu.make_async_copy(src, dst, in_sem.at[i])
        for i, (src, dst) in enumerate(
            ((ret_hbm, ret), (kw_hbm, kw), (vw_hbm, vw), (st_hbm, st), (og_hbm, og))
        )
    ]
    for cp in loads:
        cp.start()

    wred = GroupReduce(pos, wbuf, wr1, wr2, (w1s, w1r, w2s, w2r))
    dred = [
        GroupReduce(pos, dbuf.at[h], dr1.at[h], dr2.at[h], (d1s.at[h], d1r.at[h], d2s.at[h], d2r.at[h]))
        for h in range(2)
    ]
    partner = ((y * 4 + x) * 2 + 1 - c, z)

    barrier = pltpu.get_barrier_semaphore()
    peers = [(g, lax.rem(z + o, NZ)) for o in range(1, NZ)]
    peers.append(partner)
    for along in (True, False):
        for d in (1, -1):
            peers.append(wred.dev(along, d))
    peers.append(wred.dev(False, 2))
    for dev in peers:
        pl.semaphore_signal(barrier, inc=1, device_id=dev, device_id_type=MESH)

    loads[0].wait()

    def pair(owner):
        return pl.ds(2 * lax.rem(owner + 2 * NZ, NZ), 2)

    def block(owner):
        return mem[pair(owner)].reshape(FEAT, TOKS)

    mem[pair(z)] = (ret[0].astype(F32) + ret[1].astype(F32)).astype(BF16).reshape(2, 2, GROWS, TOKS)
    pl.semaphore_wait(barrier, len(peers))

    sent = []

    def send(src, dst, ssem, rsem, dev):
        cp = pltpu.make_async_remote_copy(
            src_ref=src, dst_ref=dst, send_sem=ssem, recv_sem=rsem, device_id=dev, device_id_type=MESH
        )
        cp.start()
        sent.append(cp)
        return cp

    ways = ((0, 1), (1, -1))
    ag = {}

    def ag_step(s):
        for i in range(2):
            for way, d in ways:
                h = i if way == 0 else 1 - i
                if s == 4 and i == 1:
                    continue
                if s > 1:
                    ag[way, s - 1, h].wait_recv()
                at = mem.at[2 * lax.rem(z - d * (s - 1) + 2 * NZ, NZ) + h]
                ag[way, s, h] = send(
                    at, at, ag_s.at[way, s - 1, h], ag_r.at[way, s - 1, h], (g, lax.rem(z + d + NZ, NZ))
                )

    def split_weights():
        for k in range(NZ):
            cols = slice(k * FEAT, (k + 1) * FEAT)
            wcol[k, 0:FEAT] = kw[0, :, cols]
            wcol[k, FEAT : 2 * FEAT] = kw[1, :, cols]
            wcol[k, 2 * FEAT :] = vw[:, cols]

    def turn_weights(lo, hi):
        def body(k, carry):
            wrow[k] = jnp.transpose(wcol[k])
            return carry

        lax.fori_loop(lo, hi, body, 0)

    def forward(owner, first=False):
        k = lax.rem(owner + 2 * NZ, NZ)
        rhs = block(owner)

        def body(j, carry):
            rows = pl.ds(pl.multiple_of(j * FEAT, 32), FEAT)
            val = jnp.dot(wcol[k, rows], rhs, preferred_element_type=F32)
            if first:
                acc[rows] = val
            else:
                acc[rows] += val
            return carry

        lax.fori_loop(0, 3, body, 0)

    def core_send(i, src, dst):
        return send(src, dst, co_s.at[i], co_r.at[i], partner)

    def mark(m, carry):
        a, b = lax.div(m, 4), lax.rem(m, 4)
        n = a * (1 + 3 * c) + b * (4 - 3 * c)
        at = lax.broadcasted_iota(jnp.int32, (TOKS, 128), 1).astype(F32)
        for side in range(2):
            for half in range(2):
                rows = at + ((2 * n + c) * OROWS + half * 128).astype(F32)
                both = (rows == id_cols[side, 0]).astype(F32) + (rows == id_cols[side, 1]).astype(F32)
                hits[a, b, side * TOKS : (side + 1) * TOKS, half * 128 : (half + 1) * 128] = both.astype(BF16)
        return carry

    def spread_ids(side, ids):
        vals = ids[...].astype(F32)
        cols = jnp.transpose(jnp.concatenate([vals] * 4, axis=0))
        for j in range(2):
            id_cols[side, j] = jnp.broadcast_to(cols[:, j : j + 1], (TOKS, 128))

    ag_step(1)
    ids_copy = core_send(0, idx_ref, idx_in)
    loads[1].wait()
    loads[2].wait()
    split_weights()
    ag_step(2)
    forward(z, True)
    forward(z - 1)
    forward(z + 1)
    loads[3].wait()
    loads[4].wait()
    for j in range(2):
        s = st[j].astype(F32)
        stat[j : j + 1] = jnp.sum(s * s, axis=0, keepdims=True)
    ids_copy.wait_recv()
    spread_ids(0, idx_ref)
    spread_ids(1, idx_in)
    turn_weights(0, 2)
    ag_step(3)
    forward(z - 2)
    forward(z + 2)
    turn_weights(2, 5)
    lax.fori_loop(0, 8, mark, 0)
    ag_step(4)
    ag[0, 3, 1].wait_recv()
    ag[1, 3, 0].wait_recv()
    forward(z - 3)
    forward(z + 3)
    turn_weights(5, 8)
    lax.fori_loop(8, CHIPS, mark, 0)
    ag[0, 4, 0].wait_recv()
    ag[1, 4, 1].wait_recv()
    forward(z + 4)

    for j in range(2):
        s = st[j].astype(F32)
        kv = acc[j * FEAT : (j + 1) * FEAT]
        stat[2 + j : 3 + j] = jnp.sum(kv * kv, axis=0, keepdims=True)
        stat[4 + j : 5 + j] = jnp.sum(s * kv, axis=0, keepdims=True)
        stat[6 + j : 7 + j] = jnp.sum(og[j].astype(F32) * acc[2 * FEAT :], axis=0, keepdims=True)

    ps = [
        send(stat, stat_in.at[o - 1], ps_s.at[o - 1], ps_r.at[o - 1], (g, lax.rem(z + o, NZ)))
        for o in range(1, NZ)
    ]
    mem_copy = core_send(1, mem.at[:, 1 - c], mem_in)
    total = stat[...]
    for o in range(1, NZ):
        ps[o - 1].wait_recv()
        total = total + stat_in[o - 1]

    root = jnp.sqrt(F32(WIDE))
    value_cot = None
    for j in range(2):
        state_rs = lax.rsqrt(total[j : j + 1] / WIDE + EPS_NORM)
        key_rs = lax.rsqrt(total[2 + j : 3 + j] / WIDE + EPS_NORM)
        scores = total[4 + j : 5 + j] * state_rs * key_rs / root
        gate = jax.nn.sigmoid(scores)
        dscore = total[6 + j : 7 + j] * gate * (1.0 - gate)
        lead = key_rs * dscore / root
        back = key_rs * scores / root
        kv = acc[j * FEAT : (j + 1) * FEAT]
        cot[j * FEAT : (j + 1) * FEAT] = (lead * (st[j].astype(F32) * state_rs - kv * back)).astype(BF16)
        part = gate * og[j].astype(F32)
        value_cot = part if value_cot is None else value_cot + part
    cot[2 * FEAT :] = value_cot.astype(BF16)

    cot_copy = core_send(2, cot, cot_in)
    zr = {}

    def term(dest, h, t):
        k = lax.rem(dest + 2 * NZ, NZ)
        return jnp.dot(
            wrow[k, h * HALF : (h + 1) * HALF],
            cot[:, t * (TOKS // 2) : (t + 1) * (TOKS // 2)],
            preferred_element_type=F32,
        )

    def z_send(way, s, h, t):
        d = 1 - 2 * way
        val = term(z + d * (5 - s), h, t)
        if (way, s - 1, h, t) in zr:
            zr[way, s - 1, h, t].wait_recv()
            val = val + zrecv[h, way, s - 2, t].astype(F32)
        zsend[h, way, s - 1, t] = val.astype(BF16)
        zr[way, s, h, t] = send(
            zsend.at[h, way, s - 1, t], zrecv.at[h, way, s - 1, t],
            zs_s.at[h, way, s - 1, t], zs_r.at[h, way, s - 1, t],
            (g, lax.rem(z + d + NZ, NZ)),
        )

    def z_long(s, h):
        for way in (0, 1):
            z_send(way, s, h, way)

    def z_short(s, h):
        for way in (0, 1):
            z_send(way, s, h, 1 - way)

    def z_end(h):
        for t in range(2):
            val = term(z, h, t)
            for way in (0, 1):
                zr[way, 4, h, t].wait_recv()
                val = val + zrecv[h, way, 3, t].astype(F32)
            mc[h, :, t * (TOKS // 2) : (t + 1) * (TOKS // 2)] = val.astype(BF16)
        return core_send(3 + h, mc.at[h, :, 0:TOKS], mc.at[h, :, TOKS : 2 * TOKS])

    def weight_rows(i):
        rows = pl.ds(4 * i, 4)
        val = lax.dot_general(
            mem[rows, c].reshape(4 * GROWS, TOKS), cot[...], NT, preferred_element_type=F32
        ) + lax.dot_general(
            mem_in[rows].reshape(4 * GROWS, TOKS), cot_in[...], NT, preferred_element_type=F32
        )
        wbuf[rows] = val.astype(BF16).reshape(4, GROWS, OUTS)

    def dense(h, da):
        a = lax.rem(dred[h].pa + da + 4, 4)
        left = mc[h]
        for b in range(4):
            n = a * (1 + 3 * c) + b * (4 - 3 * c)
            dbuf[h, n] = jnp.dot(left, hits[a, b], preferred_element_type=F32).astype(BF16)

    z_long(1, 0)
    z_short(2, 0)
    mem_copy.wait_recv()
    cot_copy.wait_recv()
    weight_rows(0)
    z_long(2, 0)
    weight_rows(1)
    z_short(3, 0)
    weight_rows(2)
    z_long(3, 0)
    weight_rows(3)
    wred.ring1_far()
    wred.ring1_near()
    z_short(4, 0)
    z_long(1, 1)
    z_long(4, 0)
    z_short(2, 1)
    wred.ring1_pass()
    z_long(2, 1)
    mc_copy = z_end(0)
    z_short(3, 1)
    mc_copy.wait_recv()
    dense(0, 2)
    dred[0].ring1_far()
    dense(0, 1)
    dense(0, -1)
    dred[0].ring1_near()
    z_long(3, 1)
    wred.cross()
    dense(0, 0)
    z_short(4, 1)
    dred[0].ring1_pass()
    z_long(4, 1)
    wred.ring1_end(3)
    dred[0].cross()
    mc_copy = z_end(1)
    mc_copy.wait_recv()
    dense(1, 2)
    dred[1].ring1_far()
    dense(1, 1)
    dense(1, -1)
    dred[1].ring1_near()
    dense(1, 0)
    dred[0].ring1_end(3)
    dred[1].ring1_pass()
    wg_out[...] = wred.ring2_end()
    squares = []

    def finish(h):
        val = dred[h].ring2_end()
        rg_out[h * HALF : (h + 1) * HALF] = val
        squares.append(jnp.sum(val * val, axis=0, keepdims=True))

    finish(0)
    dred[1].cross()
    dred[1].ring1_end(3)
    finish(1)
    squares = squares[0] + squares[1]
    rsum[...] = jnp.broadcast_to(squares, rsum.shape)
    rq = [
        send(rsum, rsum_in.at[o - 1], rs_s.at[o - 1], rs_r.at[o - 1], (g, lax.rem(z + o, NZ)))
        for o in range(1, NZ)
    ]
    total = rsum[...]
    for o in range(1, NZ):
        rq[o - 1].wait_recv()
        total = total + rsum_in[o - 1]
    rs_out[...] = total
    for cp in sent:
        cp.wait_send()
    for red in (wred, *dred):
        red.drain()


def update(wg, rg, rs, kacc, vacc, tier, mean, second, kgrad, vgrad, mean_out, second_out, step_out):
    for j in range(2):
        kgrad[j] = kacc[j] + wg[:, j * FEAT : (j + 1) * FEAT]
    vgrad[...] = vacc[...] + wg[:, 2 * FEAT :]
    row_grad = rg[...]
    is_hot = jnp.broadcast_to(tier[...] == 1, row_grad.shape)
    old_mean, old_second = mean[...], second[...]
    mean_hot = 0.9 * old_mean + 0.1 * row_grad
    second_hot = 0.95 * old_second + 0.05 * row_grad * row_grad
    step_hot = mean_hot / FIRST_BIAS / (jnp.sqrt(second_hot / SECOND_BIAS) + EPS_ADAM)
    step_cold = row_grad * lax.rsqrt(rs[0:1] / WIDE + EPS_NORM)
    mean_out[...] = jnp.where(is_hot, mean_hot, old_mean)
    second_out[...] = jnp.where(is_hot, second_hot, old_second)
    step_out[...] = jnp.where(is_hot, step_hot, step_cold)


def on_device(
    retrieved, branch_states, out_grad, key_weight, value_weight, key_grad_acc, value_grad_acc,
    row_index, row_tier, adam_mean, adam_second,
):
    by_feature = functools.partial(jnp.transpose, axes=(1, 2, 0))
    any_spec = pl.BlockSpec(memory_space=pl.ANY)
    vmem = pl.BlockSpec(memory_space=pltpu.VMEM)
    dma = pltpu.SemaphoreType.DMA
    wg, rg, rs = pl.pallas_call(
        exchange,
        out_shape=(
            jax.ShapeDtypeStruct((GROWS, OUTS), F32),
            jax.ShapeDtypeStruct((FEAT, OROWS), F32),
            jax.ShapeDtypeStruct((8, OROWS), F32),
        ),
        in_specs=[any_spec] * 5 + [vmem],
        out_specs=[vmem] * 3,
        scratch_shapes=[
            pltpu.VMEM((2, FEAT, TOKS), BF16),
            pltpu.VMEM((2, FEAT, TOKS), BF16),
            pltpu.VMEM((2, FEAT, TOKS), BF16),
            pltpu.VMEM((2, FEAT, WIDE), BF16),
            pltpu.VMEM((FEAT, WIDE), BF16),
            pltpu.VMEM((NZ, OUTS, FEAT), BF16),
            pltpu.VMEM((NZ, FEAT, OUTS), BF16),
            pltpu.VMEM((CHIPS, 2, GROWS, TOKS), BF16),
            pltpu.VMEM((CHIPS, GROWS, TOKS), BF16),
            pltpu.VMEM((OUTS, TOKS), F32),
            pltpu.VMEM((OUTS, TOKS), BF16),
            pltpu.VMEM((OUTS, TOKS), BF16),
            pltpu.VMEM((8, TOKS), F32),
            pltpu.VMEM((NZ - 1, 8, TOKS), F32),
            pltpu.VMEM((2, 2, 4, 2, HALF, TOKS // 2), BF16),
            pltpu.VMEM((2, 2, 4, 2, HALF, TOKS // 2), BF16),
            pltpu.VMEM((2, HALF, 2 * TOKS), BF16),
            pltpu.VMEM((8, OROWS), F32),
            pltpu.VMEM((NZ - 1, 8, OROWS), F32),
            pltpu.VMEM((2, TOKS), jnp.int32),
            pltpu.VMEM((2, 2, TOKS, 128), F32),
            pltpu.VMEM((4, 4, 2 * TOKS, OROWS), BF16),
            pltpu.VMEM((CHIPS, GROWS, OUTS), BF16),
            pltpu.VMEM((2, 3, 2, GROWS, OUTS), BF16),
            pltpu.VMEM((3, GROWS, OUTS), BF16),
            pltpu.VMEM((2, CHIPS, HALF, OROWS), BF16),
            pltpu.VMEM((2, 2, 3, 2, HALF, OROWS), BF16),
            pltpu.VMEM((2, 3, HALF, OROWS), BF16),
            dma((5,)),
            dma((2, 4, 2)), dma((2, 4, 2)),
            dma((NZ - 1,)), dma((NZ - 1,)),
            dma((2, 2, 4, 2)), dma((2, 2, 4, 2)),
            dma((NZ - 1,)), dma((NZ - 1,)),
            dma((5,)), dma((5,)),
            dma((2, 3, 2)), dma((2, 3, 2)), dma((3,)), dma((3,)),
            dma((2, 2, 3, 2)), dma((2, 2, 3, 2)), dma((2, 3)), dma((2, 3)),
        ],
        compiler_params=pltpu.CompilerParams(
            collective_id=0, has_side_effects=True, vmem_limit_bytes=53_600_000
        ),
        name="exchange",
    )(
        by_feature(retrieved),
        by_feature(branch_states),
        by_feature(out_grad),
        jnp.transpose(key_weight, (0, 2, 1)),
        value_weight.T,
        row_index.T,
    )
    feat_rows = jax.ShapeDtypeStruct((FEAT, OROWS), F32)
    key_grad, value_grad, new_mean, new_second, row_step = pl.pallas_call(
        update,
        out_shape=(
            jax.ShapeDtypeStruct((2, GROWS, FEAT), F32),
            jax.ShapeDtypeStruct((GROWS, FEAT), F32),
            feat_rows, feat_rows, feat_rows,
        ),
        in_specs=[vmem] * 8,
        out_specs=[vmem] * 5,
        compiler_params=pltpu.CompilerParams(vmem_limit_bytes=8_000_000),
        name="update",
    )(
        wg, rg, rs, key_grad_acc, value_grad_acc, row_tier.reshape(1, OROWS), adam_mean.T, adam_second.T
    )
    return key_grad, value_grad, new_mean.T, new_second.T, row_step.T


def solution(mesh):
    return jax.shard_map(
        on_device,
        mesh=mesh,
        in_specs=(
            P("group", None, "tensor"),
            P("group", None, "tensor"),
            P("group", None, "tensor"),
            P(None, None, "tensor"),
            P(None, "tensor"),
            P(None, "group", "tensor"),
            P("group", "tensor"),
            P("group", None),
            P("group"),
            P("group", "tensor"),
            P("group", "tensor"),
        ),
        out_specs=(
            P(None, "group", "tensor"),
            P("group", "tensor"),
            P("group", "tensor"),
            P("group", "tensor"),
            P("group", "tensor"),
        ),
        check_vma=False,
    )
```

```python
import functools

import jax
import jax.numpy as jnp
from jax import lax
from jax.experimental import pallas as pl
from jax.experimental.pallas import tpu as pltpu
from jax.sharding import PartitionSpec as P

EPS_NORM = 1e-06
EPS_ADAM = 1e-08
FIRST_BIAS = 1.0 - 0.9**10
SECOND_BIAS = 1.0 - 0.95**10

MESH = pl.DeviceIdType.MESH
F32 = jnp.float32
BF16 = jnp.bfloat16
NZ = 8
NX = 4
NY = 4
CHIPS = 16
FEAT = 320
HALF = 160
TOKS = 512
WIDE = 2560
OUTS = 960
GROWS = 80
OROWS = 256

FAR_FIRST = (4, 3, 5, 2, 6, 1, 7)

NT = (((1,), (1,)), ((), ()))


class GroupReduce:
    def __init__(self, pos, buf, ring1_in, ring2_in, sems):
        self.y, self.x, self.c, self.z = pos
        self.buf, self.r1, self.r2 = buf, ring1_in, ring2_in
        self.s1, self.q1, self.s2, self.q2 = sems
        c, x, y = self.c, self.x, self.y
        self.pa = x + c * (y - x)
        self.pb = y + c * (x - y)
        self.sent = []
        self.k1, self.k2 = {}, {}

    def chip(self, da, i):
        a = lax.rem(self.pa + da + 4, 4)
        b = lax.rem(self.pb + (2, 1, -1, 0)[i] + 4, 4)
        return a * (1 + 3 * self.c) + b * (4 - 3 * self.c)

    def dev(self, along_a, d):
        c = self.c
        dx = (1 - c) if along_a else c
        dy = c if along_a else (1 - c)
        nx = lax.rem(self.x + dx * d + 4, 4)
        ny = lax.rem(self.y + dy * d + 4, 4)
        return ((ny * 4 + nx) * 2 + c, self.z)

    def send(self, src, dst, ssem, rsem, dev):
        cp = pltpu.make_async_remote_copy(
            src_ref=src, dst_ref=dst, send_sem=ssem, recv_sem=rsem, device_id=dev, device_id_type=MESH
        )
        cp.start()
        self.sent.append(cp)
        return cp

    def send1(self, way, step, i):
        d = 1 - 2 * way
        n = self.chip(2 if step == 0 else d, i)
        slot = i % 2
        self.k1[way, step, i] = self.send(
            self.buf.at[n], self.r1.at[way, step, slot], self.s1.at[way, step, slot], self.q1.at[way, step, slot],
            self.dev(True, d),
        )

    def ring1_far(self):
        self.send1(0, 0, 0)
        self.send1(1, 0, 2)
        self.send1(0, 0, 1)
        self.send1(1, 0, 3)

    def ring1_near(self):
        self.send1(0, 1, 2)
        self.send1(1, 1, 0)
        self.send1(1, 1, 1)

    def add(self, n, *terms):
        val = self.buf[n].astype(F32)
        for way, step, slot in terms:
            val = val + self.r1[way, step, slot].astype(F32)
        self.buf[n] = val.astype(BF16)

    def ring1_pass(self):
        for way, i in ((0, 0), (1, 2), (0, 1), (1, 3)):
            self.k1[way, 0, i].wait_recv()
            self.add(self.chip(1 - 2 * way, i), (way, 0, i % 2))
            self.send1(way, 2, i)
        self.send1(0, 1, 3)

    def ring1_end(self, i):
        up, down = (2, 1) if i < 2 else (1, 2)
        self.k1[0, up, i].wait_recv()
        self.k1[1, down, i].wait_recv()
        self.add(self.chip(0, i), (0, up, i % 2), (1, down, i % 2))

    def send2(self, i):
        d = (2, 1, -1)[i]
        self.k2[i] = self.send(
            self.buf.at[self.chip(0, i)], self.r2.at[i], self.s2.at[i], self.q2.at[i], self.dev(False, d)
        )

    def cross(self):
        for i in range(3):
            self.ring1_end(i)
            self.send2(i)

    def ring2_end(self):
        val = self.buf[self.chip(0, 3)].astype(F32)
        for i in range(3):
            self.k2[i].wait_recv()
            val = val + self.r2[i].astype(F32)
        return val

    def drain(self):
        for cp in self.sent:
            cp.wait_send()


def exchange(
    ret_hbm, st_hbm, og_hbm, kw_hbm, vw_hbm, idx_hbm,
    wg_out, rg_out, rs_out,
    ret, st, og, kw, vw, wcol, wrow, mem, mem_in, acc, cot, cot_in, stat, stat_in, zsend, zrecv, mc, rsum, rsum_in,
    idx_ref, idx_in, id_cols, hits, wbuf, wr1, wr2, dbuf, dr1, dr2,
    in_sem, ag_s, ag_r, ps_s, ps_r, zs_s, zs_r, rs_s, rs_r, co_s, co_r,
    w1s, w1r, w2s, w2r, d1s, d1r, d2s, d2r,
):
    g = lax.axis_index("group")
    z = lax.axis_index("tensor")
    c = lax.rem(g, 2)
    x = lax.rem(lax.div(g, 2), 4)
    y = lax.div(g, 8)
    pos = (y, x, c, z)

    loads = [
        pltpu.make_async_copy(src, dst, in_sem.at[i])
        for i, (src, dst) in enumerate(
            ((ret_hbm, ret), (kw_hbm, kw), (vw_hbm, vw), (st_hbm, st), (og_hbm, og), (idx_hbm, idx_ref))
        )
    ]
    loads[0].start()

    wred = GroupReduce(pos, wbuf, wr1, wr2, (w1s, w1r, w2s, w2r))
    dred = [
        GroupReduce(pos, dbuf.at[h], dr1.at[h], dr2.at[h], (d1s.at[h], d1r.at[h], d2s.at[h], d2r.at[h]))
        for h in range(2)
    ]
    partner = ((y * 4 + x) * 2 + 1 - c, z)

    barrier = pltpu.get_barrier_semaphore()
    peers = [(g, lax.rem(z + o, NZ)) for o in range(1, NZ)]
    peers.append(partner)
    for along in (True, False):
        for d in (1, -1):
            peers.append(wred.dev(along, d))
    peers.append(wred.dev(False, 2))
    for dev in peers:
        pl.semaphore_signal(barrier, inc=1, device_id=dev, device_id_type=MESH)

    loads[0].wait()

    def pair(owner):
        return pl.ds(2 * lax.rem(owner + 2 * NZ, NZ), 2)

    def block(owner):
        return mem[pair(owner)].reshape(FEAT, TOKS)

    mem[pair(z)] = (ret[0].astype(F32) + ret[1].astype(F32)).astype(BF16).reshape(2, 2, GROWS, TOKS)
    pl.semaphore_wait(barrier, len(peers))

    sent = []

    def send(src, dst, ssem, rsem, dev):
        cp = pltpu.make_async_remote_copy(
            src_ref=src, dst_ref=dst, send_sem=ssem, recv_sem=rsem, device_id=dev, device_id_type=MESH
        )
        cp.start()
        sent.append(cp)
        return cp

    ways = ((0, 1), (1, -1))
    ag = {}

    def ag_step(s):
        for i in range(2):
            for way, d in ways:
                h = i if way == 0 else 1 - i
                if s == 4 and i == 1:
                    continue
                if s > 1:
                    ag[way, s - 1, h].wait_recv()
                at = mem.at[2 * lax.rem(z - d * (s - 1) + 2 * NZ, NZ) + h]
                ag[way, s, h] = send(
                    at, at, ag_s.at[way, s - 1, h], ag_r.at[way, s - 1, h], (g, lax.rem(z + d + NZ, NZ))
                )

    def split_weights():
        for k in range(NZ):
            cols = slice(k * FEAT, (k + 1) * FEAT)
            wcol[k, 0:FEAT] = kw[0, :, cols]
            wcol[k, FEAT : 2 * FEAT] = kw[1, :, cols]
            wcol[k, 2 * FEAT :] = vw[:, cols]

    def turn_weights(lo, hi):
        def body(k, carry):
            wrow[k] = jnp.transpose(wcol[k])
            return carry

        lax.fori_loop(lo, hi, body, 0)

    def forward(owner, first=False):
        k = lax.rem(owner + 2 * NZ, NZ)
        rhs = block(owner)

        def body(j, carry):
            rows = pl.ds(pl.multiple_of(j * FEAT, 32), FEAT)
            val = jnp.dot(wcol[k, rows], rhs, preferred_element_type=F32)
            if first:
                acc[rows] = val
            else:
                acc[rows] += val
            return carry

        lax.fori_loop(0, 3, body, 0)

    def core_send(i, src, dst):
        return send(src, dst, co_s.at[i], co_r.at[i], partner)

    def mark(m, carry):
        a, b = lax.div(m, 4), lax.rem(m, 4)
        n = a * (1 + 3 * c) + b * (4 - 3 * c)
        at = lax.broadcasted_iota(jnp.int32, (TOKS, 128), 1).astype(F32)
        for side in range(2):
            for half in range(2):
                rows = at + ((2 * n + c) * OROWS + half * 128).astype(F32)
                both = (rows == id_cols[side, 0]).astype(F32) + (rows == id_cols[side, 1]).astype(F32)
                hits[a, b, side * TOKS : (side + 1) * TOKS, half * 128 : (half + 1) * 128] = both.astype(BF16)
        return carry

    def spread_ids(side, ids):
        vals = ids[...].astype(F32)
        cols = jnp.transpose(jnp.concatenate([vals] * 4, axis=0))
        for j in range(2):
            id_cols[side, j] = jnp.broadcast_to(cols[:, j : j + 1], (TOKS, 128))

    ag_step(1)
    for i in (5, 1, 2, 3, 4):
        loads[i].start()
    loads[5].wait()
    ids_copy = core_send(0, idx_ref, idx_in)
    loads[1].wait()
    loads[2].wait()
    split_weights()
    ag_step(2)
    forward(z, True)
    forward(z - 1)
    forward(z + 1)
    loads[3].wait()
    loads[4].wait()
    for j in range(2):
        s = st[j].astype(F32)
        stat[j : j + 1] = jnp.sum(s * s, axis=0, keepdims=True)
    ids_copy.wait_recv()
    spread_ids(0, idx_ref)
    spread_ids(1, idx_in)
    turn_weights(0, 2)
    ag_step(3)
    forward(z - 2)
    forward(z + 2)
    turn_weights(2, 5)
    lax.fori_loop(0, 8, mark, 0)
    ag_step(4)
    ag[0, 3, 1].wait_recv()
    ag[1, 3, 0].wait_recv()
    forward(z - 3)
    forward(z + 3)
    turn_weights(5, 8)
    lax.fori_loop(8, CHIPS, mark, 0)
    ag[0, 4, 0].wait_recv()
    ag[1, 4, 1].wait_recv()
    forward(z + 4)

    for j in range(2):
        s = st[j].astype(F32)
        kv = acc[j * FEAT : (j + 1) * FEAT]
        stat[2 + j : 3 + j] = jnp.sum(kv * kv, axis=0, keepdims=True)
        stat[4 + j : 5 + j] = jnp.sum(s * kv, axis=0, keepdims=True)
        stat[6 + j : 7 + j] = jnp.sum(og[j].astype(F32) * acc[2 * FEAT :], axis=0, keepdims=True)

    ps = {
        o: send(stat, stat_in.at[o - 1], ps_s.at[o - 1], ps_r.at[o - 1], (g, lax.rem(z + o, NZ)))
        for o in FAR_FIRST
    }
    mem_copy = core_send(1, mem.at[:, 1 - c], mem_in)
    total = stat[...]
    for o in range(1, NZ):
        ps[o].wait_recv()
        total = total + stat_in[o - 1]

    root = jnp.sqrt(F32(WIDE))
    value_cot = None
    for j in range(2):
        state_rs = lax.rsqrt(total[j : j + 1] / WIDE + EPS_NORM)
        key_rs = lax.rsqrt(total[2 + j : 3 + j] / WIDE + EPS_NORM)
        scores = total[4 + j : 5 + j] * state_rs * key_rs / root
        gate = jax.nn.sigmoid(scores)
        dscore = total[6 + j : 7 + j] * gate * (1.0 - gate)
        lead = key_rs * dscore / root
        back = key_rs * scores / root
        kv = acc[j * FEAT : (j + 1) * FEAT]
        cot[j * FEAT : (j + 1) * FEAT] = (lead * (st[j].astype(F32) * state_rs - kv * back)).astype(BF16)
        part = gate * og[j].astype(F32)
        value_cot = part if value_cot is None else value_cot + part
    cot[2 * FEAT :] = value_cot.astype(BF16)

    cot_copy = core_send(2, cot, cot_in)
    zr = {}

    def term(dest, h, t):
        k = lax.rem(dest + 2 * NZ, NZ)
        return jnp.dot(
            wrow[k, h * HALF : (h + 1) * HALF],
            cot[:, t * (TOKS // 2) : (t + 1) * (TOKS // 2)],
            preferred_element_type=F32,
        )

    def z_send(way, s, h, t):
        d = 1 - 2 * way
        val = term(z + d * (5 - s), h, t)
        if (way, s - 1, h, t) in zr:
            zr[way, s - 1, h, t].wait_recv()
            val = val + zrecv[h, way, s - 2, t].astype(F32)
        zsend[h, way, s - 1, t] = val.astype(BF16)
        zr[way, s, h, t] = send(
            zsend.at[h, way, s - 1, t], zrecv.at[h, way, s - 1, t],
            zs_s.at[h, way, s - 1, t], zs_r.at[h, way, s - 1, t],
            (g, lax.rem(z + d + NZ, NZ)),
        )

    def z_long(s, h):
        for way in (0, 1):
            z_send(way, s, h, way)

    def z_short(s, h):
        for way in (0, 1):
            z_send(way, s, h, 1 - way)

    def z_end(h):
        for t in range(2):
            val = term(z, h, t)
            for way in (0, 1):
                zr[way, 4, h, t].wait_recv()
                val = val + zrecv[h, way, 3, t].astype(F32)
            mc[h, :, t * (TOKS // 2) : (t + 1) * (TOKS // 2)] = val.astype(BF16)
        return core_send(3 + h, mc.at[h, :, 0:TOKS], mc.at[h, :, TOKS : 2 * TOKS])

    def weight_rows(i):
        rows = pl.ds(4 * i, 4)
        val = lax.dot_general(
            mem[rows, c].reshape(4 * GROWS, TOKS), cot[...], NT, preferred_element_type=F32
        ) + lax.dot_general(
            mem_in[rows].reshape(4 * GROWS, TOKS), cot_in[...], NT, preferred_element_type=F32
        )
        wbuf[rows] = val.astype(BF16).reshape(4, GROWS, OUTS)

    def dense(h, da):
        a = lax.rem(dred[h].pa + da + 4, 4)
        left = mc[h]
        for b in range(4):
            n = a * (1 + 3 * c) + b * (4 - 3 * c)
            dbuf[h, n] = jnp.dot(left, hits[a, b], preferred_element_type=F32).astype(BF16)

    z_long(1, 0)
    z_short(2, 0)
    mem_copy.wait_recv()
    cot_copy.wait_recv()
    weight_rows(0)
    z_long(2, 0)
    weight_rows(1)
    z_short(3, 0)
    weight_rows(2)
    z_long(3, 0)
    weight_rows(3)
    wred.ring1_far()
    wred.ring1_near()
    z_short(4, 0)
    z_long(1, 1)
    z_long(4, 0)
    z_short(2, 1)
    wred.ring1_pass()
    z_long(2, 1)
    mc_copy = z_end(0)
    z_short(3, 1)
    mc_copy.wait_recv()
    dense(0, 2)
    dred[0].ring1_far()
    dense(0, 1)
    dense(0, -1)
    dred[0].ring1_near()
    z_long(3, 1)
    wred.cross()
    dense(0, 0)
    z_short(4, 1)
    dred[0].ring1_pass()
    z_long(4, 1)
    wred.ring1_end(3)
    dred[0].cross()
    mc_copy = z_end(1)
    mc_copy.wait_recv()
    dense(1, 2)
    dred[1].ring1_far()
    dense(1, 1)
    dense(1, -1)
    dred[1].ring1_near()
    dense(1, 0)
    dred[0].ring1_end(3)
    dred[1].ring1_pass()
    wg_out[...] = wred.ring2_end()
    squares = []

    def finish(h):
        val = dred[h].ring2_end()
        rg_out[h * HALF : (h + 1) * HALF] = val
        squares.append(jnp.sum(val * val, axis=0, keepdims=True))

    finish(0)
    dred[1].cross()
    dred[1].ring1_end(3)
    finish(1)
    squares = squares[0] + squares[1]
    rsum[...] = jnp.broadcast_to(squares, rsum.shape)
    rq = {
        o: send(rsum, rsum_in.at[o - 1], rs_s.at[o - 1], rs_r.at[o - 1], (g, lax.rem(z + o, NZ)))
        for o in FAR_FIRST
    }
    total = rsum[...]
    for o in range(1, NZ):
        rq[o].wait_recv()
        total = total + rsum_in[o - 1]
    rs_out[...] = total
    for cp in sent:
        cp.wait_send()
    for red in (wred, *dred):
        red.drain()


def update(wg, rg, rs, kacc, vacc, tier, mean, second, kgrad, vgrad, mean_out, second_out, step_out):
    for j in range(2):
        kgrad[j] = kacc[j] + wg[:, j * FEAT : (j + 1) * FEAT]
    vgrad[...] = vacc[...] + wg[:, 2 * FEAT :]
    row_grad = rg[...]
    is_hot = jnp.broadcast_to(tier[...] == 1, row_grad.shape)
    old_mean, old_second = mean[...], second[...]
    mean_hot = 0.9 * old_mean + 0.1 * row_grad
    second_hot = 0.95 * old_second + 0.05 * row_grad * row_grad
    step_hot = mean_hot / FIRST_BIAS / (jnp.sqrt(second_hot / SECOND_BIAS) + EPS_ADAM)
    step_cold = row_grad * lax.rsqrt(rs[0:1] / WIDE + EPS_NORM)
    mean_out[...] = jnp.where(is_hot, mean_hot, old_mean)
    second_out[...] = jnp.where(is_hot, second_hot, old_second)
    step_out[...] = jnp.where(is_hot, step_hot, step_cold)


def on_device(
    retrieved, branch_states, out_grad, key_weight, value_weight, key_grad_acc, value_grad_acc,
    row_index, row_tier, adam_mean, adam_second,
):
    by_feature = functools.partial(jnp.transpose, axes=(1, 2, 0))
    in_hbm = pl.BlockSpec(memory_space=pltpu.HBM)
    vmem = pl.BlockSpec(memory_space=pltpu.VMEM)
    dma = pltpu.SemaphoreType.DMA
    wg, rg, rs = pl.pallas_call(
        exchange,
        out_shape=(
            jax.ShapeDtypeStruct((GROWS, OUTS), F32),
            jax.ShapeDtypeStruct((FEAT, OROWS), F32),
            jax.ShapeDtypeStruct((8, OROWS), F32),
        ),
        in_specs=[in_hbm] * 6,
        out_specs=[vmem] * 3,
        scratch_shapes=[
            pltpu.VMEM((2, FEAT, TOKS), BF16),
            pltpu.VMEM((2, FEAT, TOKS), BF16),
            pltpu.VMEM((2, FEAT, TOKS), BF16),
            pltpu.VMEM((2, FEAT, WIDE), BF16),
            pltpu.VMEM((FEAT, WIDE), BF16),
            pltpu.VMEM((NZ, OUTS, FEAT), BF16),
            pltpu.VMEM((NZ, FEAT, OUTS), BF16),
            pltpu.VMEM((CHIPS, 2, GROWS, TOKS), BF16),
            pltpu.VMEM((CHIPS, GROWS, TOKS), BF16),
            pltpu.VMEM((OUTS, TOKS), F32),
            pltpu.VMEM((OUTS, TOKS), BF16),
            pltpu.VMEM((OUTS, TOKS), BF16),
            pltpu.VMEM((8, TOKS), F32),
            pltpu.VMEM((NZ - 1, 8, TOKS), F32),
            pltpu.VMEM((2, 2, 4, 2, HALF, TOKS // 2), BF16),
            pltpu.VMEM((2, 2, 4, 2, HALF, TOKS // 2), BF16),
            pltpu.VMEM((2, HALF, 2 * TOKS), BF16),
            pltpu.VMEM((8, OROWS), F32),
            pltpu.VMEM((NZ - 1, 8, OROWS), F32),
            pltpu.VMEM((2, TOKS), jnp.int32),
            pltpu.VMEM((2, TOKS), jnp.int32),
            pltpu.VMEM((2, 2, TOKS, 128), F32),
            pltpu.VMEM((4, 4, 2 * TOKS, OROWS), BF16),
            pltpu.VMEM((CHIPS, GROWS, OUTS), BF16),
            pltpu.VMEM((2, 3, 2, GROWS, OUTS), BF16),
            pltpu.VMEM((3, GROWS, OUTS), BF16),
            pltpu.VMEM((2, CHIPS, HALF, OROWS), BF16),
            pltpu.VMEM((2, 2, 3, 2, HALF, OROWS), BF16),
            pltpu.VMEM((2, 3, HALF, OROWS), BF16),
            dma((6,)),
            dma((2, 4, 2)), dma((2, 4, 2)),
            dma((NZ - 1,)), dma((NZ - 1,)),
            dma((2, 2, 4, 2)), dma((2, 2, 4, 2)),
            dma((NZ - 1,)), dma((NZ - 1,)),
            dma((5,)), dma((5,)),
            dma((2, 3, 2)), dma((2, 3, 2)), dma((3,)), dma((3,)),
            dma((2, 2, 3, 2)), dma((2, 2, 3, 2)), dma((2, 3)), dma((2, 3)),
        ],
        compiler_params=pltpu.CompilerParams(
            collective_id=0, has_side_effects=True, vmem_limit_bytes=55_400_000
        ),
        name="exchange",
    )(
        by_feature(retrieved),
        by_feature(branch_states),
        by_feature(out_grad),
        jnp.transpose(key_weight, (0, 2, 1)),
        value_weight.T,
        row_index.T,
    )
    feat_rows = jax.ShapeDtypeStruct((FEAT, OROWS), F32)
    key_grad, value_grad, new_mean, new_second, row_step = pl.pallas_call(
        update,
        out_shape=(
            jax.ShapeDtypeStruct((2, GROWS, FEAT), F32),
            jax.ShapeDtypeStruct((GROWS, FEAT), F32),
            feat_rows, feat_rows, feat_rows,
        ),
        in_specs=[vmem] * 8,
        out_specs=[vmem] * 5,
        compiler_params=pltpu.CompilerParams(vmem_limit_bytes=8_000_000),
        name="update",
    )(
        wg, rg, rs, key_grad_acc, value_grad_acc, row_tier.reshape(1, OROWS), adam_mean.T, adam_second.T
    )
    return key_grad, value_grad, new_mean.T, new_second.T, row_step.T


def solution(mesh):
    return jax.shard_map(
        on_device,
        mesh=mesh,
        in_specs=(
            P("group", None, "tensor"),
            P("group", None, "tensor"),
            P("group", None, "tensor"),
            P(None, None, "tensor"),
            P(None, "tensor"),
            P(None, "group", "tensor"),
            P("group", "tensor"),
            P("group", None),
            P("group"),
            P("group", "tensor"),
            P("group", "tensor"),
        ),
        out_specs=(
            P(None, "group", "tensor"),
            P("group", "tensor"),
            P("group", "tensor"),
            P("group", "tensor"),
            P("group", "tensor"),
        ),
        check_vma=False,
    )
```

```python
import functools

import jax
import jax.numpy as jnp
from jax import lax
from jax.experimental import pallas as pl
from jax.experimental.pallas import tpu as pltpu
from jax.sharding import PartitionSpec as P

EPS_NORM = 1e-06
EPS_ADAM = 1e-08
FIRST_BIAS = 1.0 - 0.9**10
SECOND_BIAS = 1.0 - 0.95**10

MESH = pl.DeviceIdType.MESH
F32 = jnp.float32
BF16 = jnp.bfloat16
NZ = 8
NX = 4
NY = 4
CHIPS = 16
FEAT = 320
HALF = 160
TOKS = 512
WIDE = 2560
OUTS = 960
GROWS = 80
OROWS = 256

FAR_FIRST = (4, 3, 5, 2, 6, 1, 7)

NT = (((1,), (1,)), ((), ()))


class GroupReduce:
    def __init__(self, pos, buf, ring1_in, ring2_in, sems):
        self.y, self.x, self.c, self.z = pos
        self.buf, self.r1, self.r2 = buf, ring1_in, ring2_in
        self.s1, self.q1, self.s2, self.q2 = sems
        c, x, y = self.c, self.x, self.y
        self.pa = x + c * (y - x)
        self.pb = y + c * (x - y)
        self.sent = []
        self.k1, self.k2 = {}, {}

    def chip(self, da, i):
        a = lax.rem(self.pa + da + 4, 4)
        b = lax.rem(self.pb + (2, 1, -1, 0)[i] + 4, 4)
        return a * (1 + 3 * self.c) + b * (4 - 3 * self.c)

    def dev(self, along_a, d):
        c = self.c
        dx = (1 - c) if along_a else c
        dy = c if along_a else (1 - c)
        nx = lax.rem(self.x + dx * d + 4, 4)
        ny = lax.rem(self.y + dy * d + 4, 4)
        return ((ny * 4 + nx) * 2 + c, self.z)

    def send(self, src, dst, ssem, rsem, dev):
        cp = pltpu.make_async_remote_copy(
            src_ref=src, dst_ref=dst, send_sem=ssem, recv_sem=rsem, device_id=dev, device_id_type=MESH
        )
        cp.start()
        self.sent.append(cp)
        return cp

    def send1(self, way, step, i):
        d = 1 - 2 * way
        n = self.chip(2 if step == 0 else d, i)
        slot = i % 2
        self.k1[way, step, i] = self.send(
            self.buf.at[n], self.r1.at[way, step, slot], self.s1.at[way, step, slot], self.q1.at[way, step, slot],
            self.dev(True, d),
        )

    def ring1_far(self):
        self.send1(0, 0, 0)
        self.send1(1, 0, 2)
        self.send1(0, 0, 1)
        self.send1(1, 0, 3)

    def ring1_near(self):
        self.send1(0, 1, 2)
        self.send1(1, 1, 0)
        self.send1(1, 1, 1)

    def add(self, n, *terms):
        val = self.buf[n].astype(F32)
        for way, step, slot in terms:
            val = val + self.r1[way, step, slot].astype(F32)
        self.buf[n] = val.astype(BF16)

    def ring1_pass(self):
        for way, i in ((0, 0), (1, 2), (0, 1), (1, 3)):
            self.k1[way, 0, i].wait_recv()
            self.add(self.chip(1 - 2 * way, i), (way, 0, i % 2))
            self.send1(way, 2, i)
        self.send1(0, 1, 3)

    def ring1_end(self, i):
        up, down = (2, 1) if i < 2 else (1, 2)
        self.k1[0, up, i].wait_recv()
        self.k1[1, down, i].wait_recv()
        self.add(self.chip(0, i), (0, up, i % 2), (1, down, i % 2))

    def send2(self, i):
        d = (2, 1, -1)[i]
        self.k2[i] = self.send(
            self.buf.at[self.chip(0, i)], self.r2.at[i], self.s2.at[i], self.q2.at[i], self.dev(False, d)
        )

    def cross(self):
        for i in range(3):
            self.ring1_end(i)
            self.send2(i)

    def ring2_end(self):
        val = self.buf[self.chip(0, 3)].astype(F32)
        for i in range(3):
            self.k2[i].wait_recv()
            val = val + self.r2[i].astype(F32)
        return val

    def drain(self):
        for cp in self.sent:
            cp.wait_send()


def exchange(
    ret_hbm, st_hbm, og_hbm, kw_hbm, vw_hbm, idx_hbm,
    wg_out, rg_out, rs_out,
    ret, st, og, kw, vw, wcol, wrow, mem, mem_in, acc, cot, cot_in, stat, stat_in, zsend, zrecv, mc, rsum, rsum_in,
    idx_ref, idx_in, id_cols, hits, wbuf, wr1, wr2, dbuf, dr1, dr2,
    in_sem, ag_s, ag_r, ps_s, ps_r, zs_s, zs_r, rs_s, rs_r, co_s, co_r,
    w1s, w1r, w2s, w2r, d1s, d1r, d2s, d2r,
):
    g = lax.axis_index("group")
    z = lax.axis_index("tensor")
    c = lax.rem(g, 2)
    x = lax.rem(lax.div(g, 2), 4)
    y = lax.div(g, 8)
    pos = (y, x, c, z)

    loads = [
        pltpu.make_async_copy(src, dst, in_sem.at[i])
        for i, (src, dst) in enumerate(
            ((ret_hbm, ret), (kw_hbm, kw), (vw_hbm, vw), (st_hbm, st), (og_hbm, og), (idx_hbm, idx_ref))
        )
    ]
    loads[0].start()

    wred = GroupReduce(pos, wbuf, wr1, wr2, (w1s, w1r, w2s, w2r))
    dred = [
        GroupReduce(pos, dbuf.at[h], dr1.at[h], dr2.at[h], (d1s.at[h], d1r.at[h], d2s.at[h], d2r.at[h]))
        for h in range(2)
    ]
    partner = ((y * 4 + x) * 2 + 1 - c, z)

    barrier = pltpu.get_barrier_semaphore()
    peers = [(g, lax.rem(z + o, NZ)) for o in range(1, NZ)]
    peers.append(partner)
    for along in (True, False):
        for d in (1, -1):
            peers.append(wred.dev(along, d))
    peers.append(wred.dev(False, 2))
    for dev in peers:
        pl.semaphore_signal(barrier, inc=1, device_id=dev, device_id_type=MESH)

    loads[0].wait()

    def pair(owner):
        return pl.ds(2 * lax.rem(owner + 2 * NZ, NZ), 2)

    def block(owner):
        return mem[pair(owner)].reshape(FEAT, TOKS)

    mem[pair(z)] = (ret[0].astype(F32) + ret[1].astype(F32)).astype(BF16).reshape(2, 2, GROWS, TOKS)
    pl.semaphore_wait(barrier, len(peers))

    sent = []

    def send(src, dst, ssem, rsem, dev):
        cp = pltpu.make_async_remote_copy(
            src_ref=src, dst_ref=dst, send_sem=ssem, recv_sem=rsem, device_id=dev, device_id_type=MESH
        )
        cp.start()
        sent.append(cp)
        return cp

    ways = ((0, 1), (1, -1))
    ag = {}

    def ag_step(s):
        for i in range(2):
            for way, d in ways:
                h = i if way == 0 else 1 - i
                if s == 4 and i == 1:
                    continue
                if s > 1:
                    ag[way, s - 1, h].wait_recv()
                at = mem.at[2 * lax.rem(z - d * (s - 1) + 2 * NZ, NZ) + h]
                ag[way, s, h] = send(
                    at, at, ag_s.at[way, s - 1, h], ag_r.at[way, s - 1, h], (g, lax.rem(z + d + NZ, NZ))
                )

    def split_weights():
        for k in range(NZ):
            cols = slice(k * FEAT, (k + 1) * FEAT)
            wcol[k, 0:FEAT] = kw[0, :, cols]
            wcol[k, FEAT : 2 * FEAT] = kw[1, :, cols]
            wcol[k, 2 * FEAT :] = vw[:, cols]

    def turn_weights(lo, hi):
        def body(k, carry):
            wrow[k] = jnp.transpose(wcol[k])
            return carry

        lax.fori_loop(lo, hi, body, 0)

    def forward(owner, first=False):
        k = lax.rem(owner + 2 * NZ, NZ)
        rhs = block(owner)

        def body(j, carry):
            rows = pl.ds(pl.multiple_of(j * FEAT, 32), FEAT)
            val = jnp.dot(wcol[k, rows], rhs, preferred_element_type=F32)
            if first:
                acc[rows] = val
            else:
                acc[rows] += val
            return carry

        lax.fori_loop(0, 3, body, 0)

    def core_send(i, src, dst):
        return send(src, dst, co_s.at[i], co_r.at[i], partner)

    def mark(m, carry):
        a, b = lax.div(m, 4), lax.rem(m, 4)
        n = a * (1 + 3 * c) + b * (4 - 3 * c)
        at = lax.broadcasted_iota(jnp.int32, (TOKS, 128), 1).astype(F32)
        for side in range(2):
            for half in range(2):
                rows = at + ((2 * n + c) * OROWS + half * 128).astype(F32)
                both = (rows == id_cols[side, 0]).astype(F32) + (rows == id_cols[side, 1]).astype(F32)
                hits[a, b, side * TOKS : (side + 1) * TOKS, half * 128 : (half + 1) * 128] = both.astype(BF16)
        return carry

    def spread_ids(side, ids):
        vals = ids[...].astype(F32)
        cols = jnp.transpose(jnp.concatenate([vals] * 4, axis=0))
        for j in range(2):
            id_cols[side, j] = jnp.broadcast_to(cols[:, j : j + 1], (TOKS, 128))

    ag_step(1)
    for i in (5, 1, 2, 3, 4):
        loads[i].start()
    loads[5].wait()
    ids_copy = core_send(0, idx_ref, idx_in)
    loads[1].wait()
    loads[2].wait()
    split_weights()
    ag_step(2)
    forward(z, True)
    forward(z - 1)
    forward(z + 1)
    loads[3].wait()
    loads[4].wait()
    for j in range(2):
        s = st[j].astype(F32)
        stat[j : j + 1] = jnp.sum(s * s, axis=0, keepdims=True)
    ids_copy.wait_recv()
    spread_ids(0, idx_ref)
    spread_ids(1, idx_in)
    turn_weights(0, 2)
    ag_step(3)
    forward(z - 2)
    forward(z + 2)
    turn_weights(2, 5)
    lax.fori_loop(0, 8, mark, 0)
    ag_step(4)
    ag[0, 3, 1].wait_recv()
    ag[1, 3, 0].wait_recv()
    forward(z - 3)
    forward(z + 3)
    turn_weights(5, 8)
    lax.fori_loop(8, CHIPS, mark, 0)
    ag[0, 4, 0].wait_recv()
    ag[1, 4, 1].wait_recv()
    forward(z + 4)

    for j in range(2):
        s = st[j].astype(F32)
        kv = acc[j * FEAT : (j + 1) * FEAT]
        stat[2 + j : 3 + j] = jnp.sum(kv * kv, axis=0, keepdims=True)
        stat[4 + j : 5 + j] = jnp.sum(s * kv, axis=0, keepdims=True)
        stat[6 + j : 7 + j] = jnp.sum(og[j].astype(F32) * acc[2 * FEAT :], axis=0, keepdims=True)

    ps = {
        o: send(stat, stat_in.at[o - 1], ps_s.at[o - 1], ps_r.at[o - 1], (g, lax.rem(z + o, NZ)))
        for o in FAR_FIRST
    }
    mem_copy = core_send(1, mem.at[:, 1 - c], mem_in)
    total = stat[...]
    for o in range(1, NZ):
        ps[o].wait_recv()
        total = total + stat_in[o - 1]

    root = jnp.sqrt(F32(WIDE))
    value_cot = None
    for j in range(2):
        state_rs = lax.rsqrt(total[j : j + 1] / WIDE + EPS_NORM)
        key_rs = lax.rsqrt(total[2 + j : 3 + j] / WIDE + EPS_NORM)
        scores = total[4 + j : 5 + j] * state_rs * key_rs / root
        gate = jax.nn.sigmoid(scores)
        dscore = total[6 + j : 7 + j] * gate * (1.0 - gate)
        lead = key_rs * dscore / root
        back = key_rs * scores / root
        kv = acc[j * FEAT : (j + 1) * FEAT]
        cot[j * FEAT : (j + 1) * FEAT] = (lead * (st[j].astype(F32) * state_rs - kv * back)).astype(BF16)
        part = gate * og[j].astype(F32)
        value_cot = part if value_cot is None else value_cot + part
    cot[2 * FEAT :] = value_cot.astype(BF16)

    cot_copy = core_send(2, cot, cot_in)
    zr = {}

    def term(dest, h, t):
        k = lax.rem(dest + 2 * NZ, NZ)
        return jnp.dot(
            wrow[k, h * HALF : (h + 1) * HALF],
            cot[:, t * (TOKS // 2) : (t + 1) * (TOKS // 2)],
            preferred_element_type=F32,
        )

    def z_send(way, s, h, t):
        d = 1 - 2 * way
        val = term(z + d * (5 - s), h, t)
        if (way, s - 1, h, t) in zr:
            zr[way, s - 1, h, t].wait_recv()
            val = val + zrecv[h, way, s - 2, t].astype(F32)
        zsend[h, way, s - 1, t] = val.astype(BF16)
        zr[way, s, h, t] = send(
            zsend.at[h, way, s - 1, t], zrecv.at[h, way, s - 1, t],
            zs_s.at[h, way, s - 1, t], zs_r.at[h, way, s - 1, t],
            (g, lax.rem(z + d + NZ, NZ)),
        )

    def z_long(s, h):
        for way in (0, 1):
            z_send(way, s, h, way)

    def z_short(s, h):
        for way in (0, 1):
            z_send(way, s, h, 1 - way)

    def z_end(h):
        for t in range(2):
            val = term(z, h, t)
            for way in (0, 1):
                zr[way, 4, h, t].wait_recv()
                val = val + zrecv[h, way, 3, t].astype(F32)
            mc[h, :, t * (TOKS // 2) : (t + 1) * (TOKS // 2)] = val.astype(BF16)
        return core_send(3 + h, mc.at[h, :, 0:TOKS], mc.at[h, :, TOKS : 2 * TOKS])

    def weight_rows(i):
        rows = pl.ds(4 * i, 4)
        val = lax.dot_general(
            mem[rows, c].reshape(4 * GROWS, TOKS), cot[...], NT, preferred_element_type=F32
        ) + lax.dot_general(
            mem_in[rows].reshape(4 * GROWS, TOKS), cot_in[...], NT, preferred_element_type=F32
        )
        wbuf[rows] = val.astype(BF16).reshape(4, GROWS, OUTS)

    def dense(h, da):
        a = lax.rem(dred[h].pa + da + 4, 4)
        left = mc[h]
        for b in range(4):
            n = a * (1 + 3 * c) + b * (4 - 3 * c)
            dbuf[h, n] = jnp.dot(left, hits[a, b], preferred_element_type=F32).astype(BF16)

    z_long(1, 0)
    z_short(2, 0)
    z_long(2, 0)
    mem_copy.wait_recv()
    cot_copy.wait_recv()
    weight_rows(0)
    weight_rows(1)
    z_short(3, 0)
    weight_rows(2)
    z_long(3, 0)
    weight_rows(3)
    wred.ring1_far()
    wred.ring1_near()
    z_short(4, 0)
    z_long(1, 1)
    z_long(4, 0)
    z_short(2, 1)
    wred.ring1_pass()
    z_long(2, 1)
    mc_copy = z_end(0)
    z_short(3, 1)
    mc_copy.wait_recv()
    dense(0, 2)
    dred[0].ring1_far()
    z_long(3, 1)
    dense(0, 1)
    dense(0, -1)
    dred[0].ring1_near()
    z_short(4, 1)
    wred.cross()
    z_long(4, 1)
    dense(0, 0)
    dred[0].ring1_pass()
    mc_copy = z_end(1)
    wred.ring1_end(3)
    dred[0].cross()
    mc_copy.wait_recv()
    dense(1, 2)
    dred[1].ring1_far()
    dense(1, 1)
    dense(1, -1)
    dred[1].ring1_near()
    dense(1, 0)
    dred[0].ring1_end(3)
    dred[1].ring1_pass()
    wg_out[...] = wred.ring2_end()
    squares = []

    def finish(h):
        val = dred[h].ring2_end()
        rg_out[h * HALF : (h + 1) * HALF] = val
        squares.append(jnp.sum(val * val, axis=0, keepdims=True))

    finish(0)
    dred[1].cross()
    dred[1].ring1_end(3)
    finish(1)
    squares = squares[0] + squares[1]
    rsum[...] = jnp.broadcast_to(squares, rsum.shape)
    rq = {
        o: send(rsum, rsum_in.at[o - 1], rs_s.at[o - 1], rs_r.at[o - 1], (g, lax.rem(z + o, NZ)))
        for o in FAR_FIRST
    }
    total = rsum[...]
    for o in range(1, NZ):
        rq[o].wait_recv()
        total = total + rsum_in[o - 1]
    rs_out[...] = total
    for cp in sent:
        cp.wait_send()
    for red in (wred, *dred):
        red.drain()


def update(wg, rg, rs, kacc, vacc, tier, mean, second, kgrad, vgrad, mean_out, second_out, step_out):
    for j in range(2):
        kgrad[j] = kacc[j] + wg[:, j * FEAT : (j + 1) * FEAT]
    vgrad[...] = vacc[...] + wg[:, 2 * FEAT :]
    row_grad = rg[...]
    is_hot = jnp.broadcast_to(tier[...] == 1, row_grad.shape)
    old_mean, old_second = mean[...], second[...]
    mean_hot = 0.9 * old_mean + 0.1 * row_grad
    second_hot = 0.95 * old_second + 0.05 * row_grad * row_grad
    step_hot = mean_hot / FIRST_BIAS / (jnp.sqrt(second_hot / SECOND_BIAS) + EPS_ADAM)
    step_cold = row_grad * lax.rsqrt(rs[0:1] / WIDE + EPS_NORM)
    mean_out[...] = jnp.where(is_hot, mean_hot, old_mean)
    second_out[...] = jnp.where(is_hot, second_hot, old_second)
    step_out[...] = jnp.where(is_hot, step_hot, step_cold)


def on_device(
    retrieved, branch_states, out_grad, key_weight, value_weight, key_grad_acc, value_grad_acc,
    row_index, row_tier, adam_mean, adam_second,
):
    by_feature = functools.partial(jnp.transpose, axes=(1, 2, 0))
    in_hbm = pl.BlockSpec(memory_space=pltpu.HBM)
    vmem = pl.BlockSpec(memory_space=pltpu.VMEM)
    dma = pltpu.SemaphoreType.DMA
    wg, rg, rs = pl.pallas_call(
        exchange,
        out_shape=(
            jax.ShapeDtypeStruct((GROWS, OUTS), F32),
            jax.ShapeDtypeStruct((FEAT, OROWS), F32),
            jax.ShapeDtypeStruct((8, OROWS), F32),
        ),
        in_specs=[in_hbm] * 6,
        out_specs=[vmem] * 3,
        scratch_shapes=[
            pltpu.VMEM((2, FEAT, TOKS), BF16),
            pltpu.VMEM((2, FEAT, TOKS), BF16),
            pltpu.VMEM((2, FEAT, TOKS), BF16),
            pltpu.VMEM((2, FEAT, WIDE), BF16),
            pltpu.VMEM((FEAT, WIDE), BF16),
            pltpu.VMEM((NZ, OUTS, FEAT), BF16),
            pltpu.VMEM((NZ, FEAT, OUTS), BF16),
            pltpu.VMEM((CHIPS, 2, GROWS, TOKS), BF16),
            pltpu.VMEM((CHIPS, GROWS, TOKS), BF16),
            pltpu.VMEM((OUTS, TOKS), F32),
            pltpu.VMEM((OUTS, TOKS), BF16),
            pltpu.VMEM((OUTS, TOKS), BF16),
            pltpu.VMEM((8, TOKS), F32),
            pltpu.VMEM((NZ - 1, 8, TOKS), F32),
            pltpu.VMEM((2, 2, 4, 2, HALF, TOKS // 2), BF16),
            pltpu.VMEM((2, 2, 4, 2, HALF, TOKS // 2), BF16),
            pltpu.VMEM((2, HALF, 2 * TOKS), BF16),
            pltpu.VMEM((8, OROWS), F32),
            pltpu.VMEM((NZ - 1, 8, OROWS), F32),
            pltpu.VMEM((2, TOKS), jnp.int32),
            pltpu.VMEM((2, TOKS), jnp.int32),
            pltpu.VMEM((2, 2, TOKS, 128), F32),
            pltpu.VMEM((4, 4, 2 * TOKS, OROWS), BF16),
            pltpu.VMEM((CHIPS, GROWS, OUTS), BF16),
            pltpu.VMEM((2, 3, 2, GROWS, OUTS), BF16),
            pltpu.VMEM((3, GROWS, OUTS), BF16),
            pltpu.VMEM((2, CHIPS, HALF, OROWS), BF16),
            pltpu.VMEM((2, 2, 3, 2, HALF, OROWS), BF16),
            pltpu.VMEM((2, 3, HALF, OROWS), BF16),
            dma((6,)),
            dma((2, 4, 2)), dma((2, 4, 2)),
            dma((NZ - 1,)), dma((NZ - 1,)),
            dma((2, 2, 4, 2)), dma((2, 2, 4, 2)),
            dma((NZ - 1,)), dma((NZ - 1,)),
            dma((5,)), dma((5,)),
            dma((2, 3, 2)), dma((2, 3, 2)), dma((3,)), dma((3,)),
            dma((2, 2, 3, 2)), dma((2, 2, 3, 2)), dma((2, 3)), dma((2, 3)),
        ],
        compiler_params=pltpu.CompilerParams(
            collective_id=0, has_side_effects=True, vmem_limit_bytes=55_400_000
        ),
        name="exchange",
    )(
        by_feature(retrieved),
        by_feature(branch_states),
        by_feature(out_grad),
        jnp.transpose(key_weight, (0, 2, 1)),
        value_weight.T,
        row_index.T,
    )
    feat_rows = jax.ShapeDtypeStruct((FEAT, OROWS), F32)
    key_grad, value_grad, new_mean, new_second, row_step = pl.pallas_call(
        update,
        out_shape=(
            jax.ShapeDtypeStruct((2, GROWS, FEAT), F32),
            jax.ShapeDtypeStruct((GROWS, FEAT), F32),
            feat_rows, feat_rows, feat_rows,
        ),
        in_specs=[vmem] * 8,
        out_specs=[vmem] * 5,
        compiler_params=pltpu.CompilerParams(vmem_limit_bytes=8_000_000),
        name="update",
    )(
        wg, rg, rs, key_grad_acc, value_grad_acc, row_tier.reshape(1, OROWS), adam_mean.T, adam_second.T
    )
    return key_grad, value_grad, new_mean.T, new_second.T, row_step.T


def solution(mesh):
    return jax.shard_map(
        on_device,
        mesh=mesh,
        in_specs=(
            P("group", None, "tensor"),
            P("group", None, "tensor"),
            P("group", None, "tensor"),
            P(None, None, "tensor"),
            P(None, "tensor"),
            P(None, "group", "tensor"),
            P("group", "tensor"),
            P("group", None),
            P("group"),
            P("group", "tensor"),
            P("group", "tensor"),
        ),
        out_specs=(
            P(None, "group", "tensor"),
            P("group", "tensor"),
            P("group", "tensor"),
            P("group", "tensor"),
            P("group", "tensor"),
        ),
        check_vma=False,
    )
```
